1024 devices in a mesh: group: 256 (over y, x, z_lo, core), member: 4 (over z_hi).
Axes of the slice: x: 4, y: 4, z: 32 (z_hi: 4, z_lo: 8; z = z_hi * 8 + z_lo), core: 2. Of those that a mesh axis runs over, the one named last changes fastest.
Arguments:
- residual: float32 [2, 4096, 128, 128], P(None, 'group', 'member'), may hold values from -6 to 6
- horiz_vectors: float32 [2, 18, 18], replicated, may hold values from -1.5 to 1.5
- horiz_values: float32 [2, 18], replicated, may hold values from 0.2 to 4
- upward_eigen_tables: float32 [8, 18, 18], replicated, may hold values from -1.5 to 1.5
- upward_eigen_values: float32 [8, 18], replicated, may hold values from 0.2 to 4
- aggregate_map: int32 [256, 8, 8], P('group', 'member'), may hold values from 0 to 4095, as said below
- coarse_inverse: float32 [4096, 4096], P('group', 'member')
Outputs:
- preconditioned: float32 [2, 4096, 128, 128], P(None, 'group', 'member')
The draws below stay inside these ranges and needn't reach their ends.
Inputs may be any that keep to these rules, and one draw needn't show every extreme that they name: `aggregate_map`: the aggregate of each element; an element's aggregate holds elements next to it; every aggregate holds some element.
All inputs are finite; a program needn't handle non-finite values.
Results may differ from the reference program's by a relative error of at most 0.0003.
Values sent between devices are 32-bit elements; how exact they have to be, the bound alone decides.
No kernel may reach another device: no remote copies, remote signals or barrier semaphores. Data moves between devices by JAX's collectives and lax.ppermute only.
A program may use at most 64 MiB of HBM per device.

```python
import math
import jax
import jax.numpy as jnp
from jax import lax

ELEMENT_POINTS = 16
EXTENDED_POINTS = 18
VECTOR_TOTAL = 2
ELEMENTS_FIRST = 256
ELEMENTS_SECOND = 8
ELEMENTS_UPWARD = 8
NX = 4096
NY = 128
NZ = 128
NC = 4096


def draw_aggregate_map(key, part):
    mesh_layout = (ELEMENTS_FIRST, ELEMENTS_SECOND, ELEMENTS_UPWARD)
    index_x = lax.broadcasted_iota(jnp.int32, mesh_layout, 0)
    index_y = lax.broadcasted_iota(jnp.int32, mesh_layout, 1)
    upward_index = lax.broadcasted_iota(jnp.int32, mesh_layout, 2)
    key_move = jax.random.fold_in(key, 11)
    key_side = jax.random.fold_in(key, 23)
    key_order = jax.random.fold_in(key, 37)
    moving = jax.random.randint(key_move, mesh_layout, 0, 4) == 0
    anchored = (index_x % 2 == 0) & (index_y % 2 == 0)
    moving = moving & jnp.logical_not(anchored)
    side = jax.random.randint(key_side, mesh_layout, 0, 4)
    step_x = jnp.where(side == 0, 1, jnp.where(side == 1, -1, 0)).astype(jnp.int32)
    step_y = jnp.where(side == 2, 1, jnp.where(side == 3, -1, 0)).astype(jnp.int32)
    step_x = jnp.where(moving, step_x, 0)
    step_y = jnp.where(moving, step_y, 0)
    shifted_first = (index_x + step_x + ELEMENTS_FIRST) % ELEMENTS_FIRST
    shifted_second = (index_y + step_y + ELEMENTS_SECOND) % ELEMENTS_SECOND
    base_label = (shifted_first // 2 * (ELEMENTS_SECOND // 2) * ELEMENTS_UPWARD + shifted_second // 2 * ELEMENTS_UPWARD + upward_index).astype(jnp.int32)
    numbering = jax.random.permutation(key_order, NC).astype(jnp.int32)
    return jnp.take(numbering, base_label.reshape(-1)).reshape(mesh_layout).astype(jnp.int32)


def draw_coarse_inverse(key, part):
    key_off = jax.random.fold_in(key, 5)
    key_diag = jax.random.fold_in(key, 7)
    spread = 6.0 / math.sqrt(NC)
    off_part = jnp.clip(jax.random.normal(key_off, (NC, NC), jnp.float32), -4.0, 4.0) * spread
    diag_part = jax.random.uniform(key_diag, (NC,), jnp.float32, 4.0, 8.0)
    row_index = lax.broadcasted_iota(jnp.int32, (NC, NC), 0)
    col_index = lax.broadcasted_iota(jnp.int32, (NC, NC), 1)
    return off_part + jnp.where(row_index == col_index, diag_part[:, None], 0.0).astype(jnp.float32)


def block_levels(stream_key, shape, cuts, low, high):
    loudness = 1.0
    for dim, shards_of in cuts:
        heights = jax.random.uniform(jax.random.fold_in(jax.random.fold_in(stream_key, 6), dim), (shards_of,), jnp.float32, low / len(cuts), high / len(cuts))
        loudness = loudness * jnp.repeat(jnp.exp(heights), shape[dim] // shards_of).reshape((-1,) + (1,) * (len(shape) - 1 - dim))
    return loudness


def centred(own_key, dims, deviation, bound, split=(), kind=jnp.bfloat16):
    array = deviation * jax.random.normal(own_key, dims, jnp.float32)
    if split:
        array = array * block_levels(own_key, dims, split, -0.22, 0.18)
    return jnp.clip(array, -bound, bound).astype(kind)


def setup_inputs(seed: int = 0) -> dict:
    key_list = jax.random.split(jax.random.key(seed), 8)
    return {
        "residual": centred(key_list[0], (VECTOR_TOTAL, NX, NY, NZ), 1.0, 6.0, ((1, 256), (2, 4)), jnp.float32),
        "horiz_vectors": centred(key_list[1], (2, EXTENDED_POINTS, EXTENDED_POINTS), EXTENDED_POINTS ** -0.5, 1.5, (), jnp.float32),
        "horiz_values": jnp.clip(jnp.exp(jax.random.uniform(key_list[2], (2, EXTENDED_POINTS), jnp.float32, math.log(0.2), math.log(4.0))), 0.2, 4.0),
        "upward_eigen_tables": centred(key_list[3], (ELEMENTS_UPWARD, EXTENDED_POINTS, EXTENDED_POINTS), EXTENDED_POINTS ** -0.5, 1.5, (), jnp.float32),
        "upward_eigen_values": jnp.clip(jnp.exp(jax.random.uniform(key_list[4], (ELEMENTS_UPWARD, EXTENDED_POINTS), jnp.float32, math.log(0.2), math.log(4.0))), 0.2, 4.0),
        "aggregate_map": draw_aggregate_map(jax.random.fold_in(key_list[7], 71), 0),
        "coarse_inverse": draw_coarse_inverse(jax.random.fold_in(key_list[7], 71), 0),
    }


def element_frames(field_in, along_axis, pieces, span):
    core_part = lax.slice_in_dim(field_in, 1, 1 + pieces * span, axis=along_axis)
    new_shape = core_part.shape[:along_axis] + (pieces, span) + core_part.shape[along_axis + 1:]
    core_part = core_part.reshape(new_shape)
    left_rim = lax.slice_in_dim(field_in, 0, pieces * span, stride=span, axis=along_axis)
    right_rim = lax.slice_in_dim(field_in, span + 1, pieces * span + 2, stride=span, axis=along_axis)
    left_rim = jnp.expand_dims(left_rim, along_axis + 1)
    right_rim = jnp.expand_dims(right_rim, along_axis + 1)
    return jnp.concatenate([left_rim, core_part, right_rim], axis=along_axis + 1)


def fdm_solve(extended_box_field, horiz_vectors, horiz_values, upward_eigen_tables, upward_eigen_values):
    highest = lax.Precision.HIGHEST
    hat = jnp.einsum('vxjykz,xa->vajykz', extended_box_field, horiz_vectors[0], precision=highest)
    hat = jnp.einsum('vajykz,yb->vajbkz', hat, horiz_vectors[1], precision=highest)
    hat = jnp.einsum('vajbkz,kzc->vajbkc', hat, upward_eigen_tables, precision=highest)
    denominator = (horiz_values[0][:, None, None, None, None]
                   + horiz_values[1][None, None, :, None, None]
                   + upward_eigen_values[None, None, None, :, :])
    scaled = hat / denominator[None]
    solved = jnp.einsum('vajbkc,kzc->vajbkz', scaled, upward_eigen_tables, precision=highest)
    solved = jnp.einsum('vajbkz,yb->vajykz', solved, horiz_vectors[1], precision=highest)
    solved = jnp.einsum('vajykz,xa->vxjykz', solved, horiz_vectors[0], precision=highest)
    return solved[:, 1:-1, :, 1:-1, :, 1:-1]


def reference(residual, horiz_vectors, horiz_values, upward_eigen_tables, upward_eigen_values, aggregate_map, coarse_inverse):
    partition_weight = float(ELEMENT_POINTS) ** -1.5

    def slab_solve(index):
        rows_x = (index * ELEMENT_POINTS - 1 + jnp.arange(EXTENDED_POINTS, dtype=jnp.int32)) % NX
        layer_sheet = jnp.take(residual, rows_x.astype(jnp.int32), axis=1)
        layer_sheet = jnp.concatenate([layer_sheet[:, :, -1:], layer_sheet, layer_sheet[:, :, :1]], axis=2)
        layer_sheet = jnp.pad(layer_sheet, ((0, 0), (0, 0), (0, 0), (1, 1)))
        extended_box_field = element_frames(element_frames(layer_sheet, 2, ELEMENTS_SECOND, ELEMENT_POINTS), 4, ELEMENTS_UPWARD, ELEMENT_POINTS)
        solved = fdm_solve(extended_box_field, horiz_vectors, horiz_values, upward_eigen_tables, upward_eigen_values)
        return solved.reshape(VECTOR_TOTAL, ELEMENT_POINTS, NY, NZ)

    subdomain_part = lax.map(slab_solve, jnp.arange(ELEMENTS_FIRST, dtype=jnp.int32))
    subdomain_part = jnp.transpose(subdomain_part, (1, 0, 2, 3, 4)).reshape(VECTOR_TOTAL, NX, NY, NZ)

    element_totals = residual.reshape(VECTOR_TOTAL, ELEMENTS_FIRST, ELEMENT_POINTS, ELEMENTS_SECOND, ELEMENT_POINTS, ELEMENTS_UPWARD, ELEMENT_POINTS).sum(axis=(2, 4, 6))
    aggregate_labels = aggregate_map.reshape(-1).astype(jnp.int32)
    coarse_rhs = partition_weight * jax.ops.segment_sum(element_totals.reshape(VECTOR_TOTAL, -1).T, aggregate_labels, num_segments=NC).T
    coarse_answer = jnp.dot(coarse_rhs, coarse_inverse.T, precision=lax.Precision.HIGHEST,
                              preferred_element_type=jnp.float32)
    update_term = partition_weight * jnp.take(coarse_answer, aggregate_labels, axis=1).reshape(VECTOR_TOTAL, ELEMENTS_FIRST, ELEMENTS_SECOND, ELEMENTS_UPWARD)
    merged_result = subdomain_part.reshape(VECTOR_TOTAL, ELEMENTS_FIRST, ELEMENT_POINTS, ELEMENTS_SECOND, ELEMENT_POINTS, ELEMENTS_UPWARD, ELEMENT_POINTS) + update_term[:, :, None, :, None, :, None]
    return merged_result.reshape(VECTOR_TOTAL, NX, NY, NZ)
```

```python
import jax
import jax.numpy as jnp
from jax import lax
from jax.experimental import pallas as pl
from jax.experimental.pallas import tpu as pltpu
from jax.sharding import Mesh, PartitionSpec as P

SPAN = 16
EXTENT = 18
WEIGHT = float(SPAN) ** -1.5
PAIRS = 336
POINTS = 336
GROUP = ("y", "x", "low", "core")
PLANE = ("y", "x", "core")
LINE = ("high", "low")
LINE_SIZE = 32
PLANE_SIZE = 32


def iota(shape, dim):
    return lax.broadcasted_iota(jnp.int32, shape, dim)


def split(value):
    high = value.astype(jnp.bfloat16)
    low = (value - high.astype(jnp.float32)).astype(jnp.bfloat16)
    return high, low


def dot3(left, right, dims):
    (lh, ll), (rh, rl) = left, right

    def one(a, b):
        return lax.dot_general(a, b, (dims, ((), ())), preferred_element_type=jnp.float32)

    return one(lh, rh) + (one(lh, rl) + one(ll, rh))


def exact(left, right, dims=((1,), (0,))):
    return lax.dot_general(
        left, right, (dims, ((), ())),
        precision=lax.Precision.HIGHEST, preferred_element_type=jnp.float32,
    )


def point_index(shape, dim):
    row = iota(shape, dim)
    own = row < 256
    plane = row < 288
    far = row >= 312
    x_side = jnp.where(row < 272, 0, EXTENT - 1)
    x = jnp.where(own, (row >> 4) + 1, jnp.where(plane, x_side, row - jnp.where(far, 312, 288)))
    y = jnp.where(own | plane, (row & 15) + 1, jnp.where(far, EXTENT - 1, 0))
    return x, y


def pair_index(shape, dim):
    pair = iota(shape, dim)
    first = (pair * 3641) >> 16
    return first, pair - EXTENT * first


def contributions_kernel(labels_ref, residual_ref, out_ref):
    out_ref[...] = jnp.zeros_like(out_ref)
    lane = iota((2, 128), 1)
    for j in range(2):
        sums = jnp.concatenate(
            [
                jnp.sum(
                    jnp.sum(residual_ref[v, :, j * SPAN : (j + 1) * SPAN, :], axis=0),
                    axis=0,
                    keepdims=True,
                )
                for v in range(2)
            ],
            axis=0,
        )
        for k in range(8):
            total = jnp.sum(jnp.where((lane >> 4) == k, sums, 0.0), axis=1, keepdims=True)
            label = labels_ref[j * 8 + k]
            block = label >> 7
            out_ref[block] += jnp.where(lane == (label & 127), total * WEIGHT, 0.0)


def local_kernel(
    residual_ref, x_low_ref, x_high_ref, y_low_ref, y_high_ref,
    horiz_ref, horiz_values_ref, upward_ref, upward_values_ref,
    out_ref, box_ref, hat_ref, line_ref, line_values_ref,
):
    line_ref[...] = jnp.zeros_like(line_ref)
    for k in range(8):
        begin = 16 * k - 1
        skip = 1 if k == 0 else 0
        stop = 17 if k == 7 else 18
        line_ref[begin + skip : begin + stop, 18 * k : 18 * k + 18] = upward_ref[k, skip:stop, :]
        line_values_ref[0:1, 18 * k : 18 * k + 18] = upward_values_ref[k : k + 1, :]
    line = line_ref[...]
    z = iota((128, 144), 0)
    layer, _ = pair_index((128, 144), 1)
    line_own = split(jnp.where((z >> 4) == layer, line, 0.0))
    line = split(line)

    x_of, y_of = point_index((POINTS, EXTENT), 0)
    mode = iota((POINTS, EXTENT), 1)
    pair_a, pair_b = pair_index((EXTENT, PAIRS), 1)
    table = iota((EXTENT, PAIRS), 0)
    pick_a = jnp.where(pair_a == table, 1.0, 0.0)
    pick_b = jnp.where((pair_b == table) & (pair_a < EXTENT), 1.0, 0.0)
    rows_x = exact(jnp.where(x_of == mode, 1.0, 0.0), exact(horiz_ref[0], pick_a))
    rows_y = exact(jnp.where(y_of == mode, 1.0, 0.0), exact(horiz_ref[1], pick_b))
    plane = split(rows_x * rows_y)
    plane_own = (plane[0][:256], plane[1][:256])

    pair_first, pair_second = pair_index((PAIRS, EXTENT), 0)
    table = iota((PAIRS, EXTENT), 1)
    values = jnp.sum(
        jnp.where(pair_first == table, horiz_values_ref[0:1, :], 0.0)
        + jnp.where(pair_second == table, horiz_values_ref[1:2, :], 0.0),
        axis=1,
        keepdims=True,
    )
    inverse = 1.0 / (values + line_values_ref[...])

    for v in range(2):
        for j in range(2):
            lanes = slice(128 * (2 * v + j), 128 * (2 * v + j + 1))
            ys = slice(j * SPAN, (j + 1) * SPAN)
            box_ref[0:256, lanes] = residual_ref[v, :, ys, :].reshape(256, 128)
            box_ref[256:272, lanes] = x_low_ref[v, 0, ys, :]
            box_ref[272:288, lanes] = x_high_ref[v, 0, ys, :]
            box_ref[304:312, lanes] = jnp.zeros((8, 128), jnp.float32)
            box_ref[328:336, lanes] = jnp.zeros((8, 128), jnp.float32)
            for begin, edge, outer in ((288, 15, y_low_ref), (312, 16, y_high_ref)):
                if (edge == 15) == (j == 0):
                    box_ref[begin : begin + 18, lanes] = outer[v, :, 0, :]
                else:
                    box_ref[begin : begin + 1, lanes] = x_low_ref[v, 0, edge : edge + 1, :]
                    box_ref[begin + 1 : begin + 17, lanes] = residual_ref[v, :, edge, :]
                    box_ref[begin + 17 : begin + 18, lanes] = x_high_ref[v, 0, edge : edge + 1, :]

    hat_ref[...] = dot3(plane, split(box_ref[...]), ((0,), (0,)))
    for part in range(4):
        lanes = slice(128 * part, 128 * (part + 1))
        hat = dot3(split(hat_ref[:, lanes]), line, ((1,), (0,)))
        back = dot3(split(hat * inverse), line_own, ((1,), (1,)))
        solved = dot3(plane_own, split(back), ((1,), (0,)))
        v, j = divmod(part, 2)
        out_ref[v, :, j * SPAN : (j + 1) * SPAN, :] = solved.reshape(SPAN, SPAN, 128)


def merge_kernel(labels_ref, local_ref, coarse_ref, out_ref):
    lane = iota((2, 128), 1)
    for j in range(2):
        update = jnp.zeros((2, 128), jnp.float32)
        for k in range(8):
            label = labels_ref[j * 8 + k]
            block = ((label >> 8) << 1) | ((label >> 4) & 1)
            place = (((label >> 5) & 7) << 4) | (label & 15)
            value = jnp.sum(
                jnp.where(lane == place, coarse_ref[block], 0.0), axis=1, keepdims=True
            )
            update = update + jnp.where((lane >> 4) == k, value * WEIGHT, 0.0)
        ys = slice(j * SPAN, (j + 1) * SPAN)
        for v in range(2):
            out_ref[v, :, ys, :] = local_ref[v, :, ys, :] + update[v : v + 1][None]


def call(kernel, out_shape, scalars, arrays, scratch=()):
    return pl.pallas_call(
        kernel,
        out_shape=jax.ShapeDtypeStruct(out_shape, jnp.float32),
        in_specs=[pl.BlockSpec(memory_space=pltpu.SMEM)] * len(scalars)
        + [pl.BlockSpec(memory_space=pltpu.VMEM)] * len(arrays),
        out_specs=pl.BlockSpec(memory_space=pltpu.VMEM),
        scratch_shapes=list(scratch),
        compiler_params=pltpu.CompilerParams(vmem_limit_bytes=40 << 20),
    )(*scalars, *arrays)


def neighbours(axis, size, low_side, high_side):
    up = [(i, (i + 1) % size) for i in range(size)]
    down = [(j, i) for i, j in up]
    return lax.ppermute(high_side, axis, up), lax.ppermute(low_side, axis, down)


def to_all(value, axes, size):
    copies = jnp.broadcast_to(value[None], (size,) + value.shape)
    return lax.all_to_all(copies, axes, 0, 0)


def on_device(
    residual, horiz_vectors, horiz_values, upward_eigen_tables, upward_eigen_values,
    aggregate_map, coarse_inverse,
):
    labels = aggregate_map.reshape(16)

    x_low, x_high = neighbours(GROUP, 256, residual[:, :1], residual[:, -1:])
    low_side = jnp.concatenate([x_low[:, :, :1], residual[:, :, :1], x_high[:, :, :1]], axis=1)
    high_side = jnp.concatenate([x_low[:, :, -1:], residual[:, :, -1:], x_high[:, :, -1:]], axis=1)
    y_low, y_high = neighbours("high", 4, low_side, high_side)

    tiles = jnp.swapaxes(coarse_inverse.reshape(16, 8, 128), 0, 1)
    tile = lax.all_to_all(tiles, "low", 0, 0).reshape(128, 128)

    parts = call(contributions_kernel, (LINE_SIZE, 2, 128), [labels], [residual])
    line_sum = lax.all_to_all(parts, LINE, 0, 0).sum(axis=0)
    rhs = to_all(line_sum, PLANE, PLANE_SIZE).sum(axis=0)
    terms = lax.dot_general(
        rhs, tile, (((1,), (1,)), ((), ())),
        precision=lax.Precision.HIGHEST, preferred_element_type=jnp.float32,
    )
    rows = to_all(terms, LINE, LINE_SIZE).sum(axis=0)
    coarse = to_all(rows, PLANE, PLANE_SIZE)

    local = call(
        local_kernel, residual.shape, [],
        [residual, x_low, x_high, y_low, y_high, horiz_vectors, horiz_values,
         upward_eigen_tables, upward_eigen_values],
        [pltpu.VMEM((POINTS, 512), jnp.float32), pltpu.VMEM((PAIRS, 512), jnp.float32),
         pltpu.VMEM((128, 144), jnp.float32), pltpu.VMEM((1, 144), jnp.float32)],
    )
    return call(merge_kernel, residual.shape, [labels], [local, coarse])


def solution(mesh):
    fine = Mesh(mesh.devices.reshape(4, 4, 8, 2, 4), ("y", "x", "low", "core", "high"))
    in_specs = (
        P(None, GROUP, "high", None),
        P(), P(), P(), P(),
        P(GROUP, "high", None),
        P(GROUP, "high"),
    )
    return jax.shard_map(
        on_device, mesh=fine, in_specs=in_specs, out_specs=in_specs[0], check_vma=False
    )
```

```python
import jax
import jax.numpy as jnp
from jax import lax
from jax.experimental import pallas as pl
from jax.experimental.pallas import tpu as pltpu
from jax.sharding import Mesh, PartitionSpec as P

SPAN = 16
EXTENT = 18
WEIGHT = float(SPAN) ** -1.5
PAIRS = 336
POINTS = 336
GROUP = ("y", "x", "low", "core")
PLANE = ("y", "x", "core")
LINE = ("high", "low")
LINE_SIZE = 32
PLANE_SIZE = 32


def iota(shape, dim):
    return lax.broadcasted_iota(jnp.int32, shape, dim)


def split(value):
    high = value.astype(jnp.bfloat16)
    low = (value - high.astype(jnp.float32)).astype(jnp.bfloat16)
    return high, low


def dot3(left, right, dims):
    (lh, ll), (rh, rl) = left, right

    def one(a, b):
        return lax.dot_general(a, b, (dims, ((), ())), preferred_element_type=jnp.float32)

    return one(lh, rh) + (one(lh, rl) + one(ll, rh))


def exact(left, right, dims=((1,), (0,))):
    return lax.dot_general(
        left, right, (dims, ((), ())),
        precision=lax.Precision.HIGHEST, preferred_element_type=jnp.float32,
    )


def point_index(shape, dim):
    row = iota(shape, dim)
    own = row < 256
    plane = row < 288
    far = row >= 312
    x_side = jnp.where(row < 272, 0, EXTENT - 1)
    x = jnp.where(own, (row >> 4) + 1, jnp.where(plane, x_side, row - jnp.where(far, 312, 288)))
    y = jnp.where(own | plane, (row & 15) + 1, jnp.where(far, EXTENT - 1, 0))
    return x, y


def pair_index(shape, dim):
    pair = iota(shape, dim)
    first = (pair * 3641) >> 16
    return first, pair - EXTENT * first


def contributions_kernel(labels_ref, residual_ref, out_ref):
    out_ref[...] = jnp.zeros_like(out_ref)
    lane = iota((2, 128), 1)
    for j in range(2):
        sums = jnp.concatenate(
            [
                jnp.sum(
                    jnp.sum(residual_ref[v, :, j * SPAN : (j + 1) * SPAN, :], axis=0),
                    axis=0,
                    keepdims=True,
                )
                for v in range(2)
            ],
            axis=0,
        )
        for k in range(8):
            total = jnp.sum(jnp.where((lane >> 4) == k, sums, 0.0), axis=1, keepdims=True)
            label = labels_ref[0, j, k]
            block = label >> 7
            out_ref[block] += jnp.where(lane == (label & 127), total * WEIGHT, 0.0)


def tiles_kernel(place_ref, matrix_ref, *out_refs):
    for flip, out_ref in enumerate(out_refs):
        begin = pl.multiple_of((place_ref[0] ^ flip) * 128, 128)
        out_ref[...] = matrix_ref[:, pl.ds(begin, 128)]


def terms_kernel(place_ref, parts_ref, *refs):
    tile_refs, out_ref = refs[:8], refs[8]
    tile = jnp.concatenate([ref[...] for ref in tile_refs], axis=0)
    rhs = jnp.sum(parts_ref[...], axis=0)
    rhs = jnp.concatenate([rhs, jnp.zeros((6, 128), jnp.float32)], axis=0)
    terms = exact(rhs, tile, ((1,), (1,)))
    lane = iota((8, 128), 1)
    for bit in range(3):
        width = SPAN << bit
        other = jnp.where(
            (lane & width) != 0, pltpu.roll(terms, width, 1), pltpu.roll(terms, 128 - width, 1)
        )
        terms = jnp.where(((place_ref[0] >> bit) & 1) != 0, other, terms)
    out_ref[...] = jnp.broadcast_to(terms[:2][None], out_ref.shape)


def local_kernel(
    residual_ref, x_low_ref, x_high_ref, y_low_ref, y_high_ref,
    horiz_ref, horiz_values_ref, upward_ref, upward_values_ref,
    out_ref, box_ref, hat_ref, line_ref, line_values_ref,
):
    line_ref[...] = jnp.zeros_like(line_ref)
    for k in range(8):
        begin = 16 * k - 1
        skip = 1 if k == 0 else 0
        stop = 17 if k == 7 else 18
        line_ref[begin + skip : begin + stop, 18 * k : 18 * k + 18] = upward_ref[k, skip:stop, :]
        line_values_ref[0:1, 18 * k : 18 * k + 18] = upward_values_ref[k : k + 1, :]
    line = line_ref[...]
    z = iota((128, 144), 0)
    layer, _ = pair_index((128, 144), 1)
    line_own = split(jnp.where((z >> 4) == layer, line, 0.0))
    line = split(line)

    x_of, y_of = point_index((POINTS, EXTENT), 0)
    mode = iota((POINTS, EXTENT), 1)
    pair_a, pair_b = pair_index((EXTENT, PAIRS), 1)
    table = iota((EXTENT, PAIRS), 0)
    pick_a = jnp.where(pair_a == table, 1.0, 0.0)
    pick_b = jnp.where((pair_b == table) & (pair_a < EXTENT), 1.0, 0.0)
    rows_x = exact(jnp.where(x_of == mode, 1.0, 0.0), exact(horiz_ref[0], pick_a))
    rows_y = exact(jnp.where(y_of == mode, 1.0, 0.0), exact(horiz_ref[1], pick_b))
    plane = split(rows_x * rows_y)
    plane_own = (plane[0][:256], plane[1][:256])

    pair_first, pair_second = pair_index((PAIRS, EXTENT), 0)
    table = iota((PAIRS, EXTENT), 1)
    values = jnp.sum(
        jnp.where(pair_first == table, horiz_values_ref[0:1, :], 0.0)
        + jnp.where(pair_second == table, horiz_values_ref[1:2, :], 0.0),
        axis=1,
        keepdims=True,
    )
    inverse = 1.0 / (values + line_values_ref[...])

    for v in range(2):
        for j in range(2):
            lanes = slice(128 * (2 * v + j), 128 * (2 * v + j + 1))
            ys = slice(j * SPAN, (j + 1) * SPAN)
            box_ref[0:256, lanes] = residual_ref[v, :, ys, :].reshape(256, 128)
            box_ref[256:272, lanes] = x_low_ref[v, 0, ys, :]
            box_ref[272:288, lanes] = x_high_ref[v, 0, ys, :]
            box_ref[304:312, lanes] = jnp.zeros((8, 128), jnp.float32)
            box_ref[328:336, lanes] = jnp.zeros((8, 128), jnp.float32)
            for begin, edge, outer in ((288, 15, y_low_ref), (312, 16, y_high_ref)):
                if (edge == 15) == (j == 0):
                    box_ref[begin : begin + 18, lanes] = outer[v, :, 0, :]
                else:
                    box_ref[begin : begin + 1, lanes] = x_low_ref[v, 0, edge : edge + 1, :]
                    box_ref[begin + 1 : begin + 17, lanes] = residual_ref[v, :, edge, :]
                    box_ref[begin + 17 : begin + 18, lanes] = x_high_ref[v, 0, edge : edge + 1, :]

    hat_ref[...] = dot3(plane, split(box_ref[...]), ((0,), (0,)))
    for part in range(4):
        lanes = slice(128 * part, 128 * (part + 1))
        hat = dot3(split(hat_ref[:, lanes]), line, ((1,), (0,)))
        back = dot3(split(hat * inverse), line_own, ((1,), (1,)))
        solved = dot3(plane_own, split(back), ((1,), (0,)))
        v, j = divmod(part, 2)
        out_ref[v, :, j * SPAN : (j + 1) * SPAN, :] = solved.reshape(SPAN, SPAN, 128)


def merge_kernel(labels_ref, local_ref, coarse_ref, out_ref):
    lane = iota((2, 128), 1)
    for j in range(2):
        update = jnp.zeros((2, 128), jnp.float32)
        for k in range(8):
            label = labels_ref[0, j, k]
            block = ((label >> 8) << 1) | ((label >> 4) & 1)
            place = (((label >> 5) & 7) << 4) | (label & 15)
            value = jnp.sum(
                jnp.where(lane == place, coarse_ref[block], 0.0), axis=1, keepdims=True
            )
            update = update + jnp.where((lane >> 4) == k, value * WEIGHT, 0.0)
        ys = slice(j * SPAN, (j + 1) * SPAN)
        for v in range(2):
            out_ref[v, :, ys, :] = local_ref[v, :, ys, :] + update[v : v + 1][None]


def call(kernel, out_shape, scalars, arrays, scratch=()):
    return pl.pallas_call(
        kernel,
        out_shape=jax.ShapeDtypeStruct(out_shape, jnp.float32),
        in_specs=[pl.BlockSpec(memory_space=pltpu.SMEM)] * len(scalars)
        + [pl.BlockSpec(memory_space=pltpu.VMEM)] * len(arrays),
        out_specs=pl.BlockSpec(memory_space=pltpu.VMEM),
        scratch_shapes=list(scratch),
        compiler_params=pltpu.CompilerParams(vmem_limit_bytes=40 << 20),
    )(*scalars, *arrays)


def neighbours(axis, size, low_side, high_side):
    up = [(i, (i + 1) % size) for i in range(size)]
    down = [(j, i) for i, j in up]
    return lax.ppermute(high_side, axis, up), lax.ppermute(low_side, axis, down)


def to_all(value, axes, size):
    copies = jnp.broadcast_to(value[None], (size,) + value.shape)
    return lax.all_to_all(copies, axes, 0, 0)


def regroup(place, matrix):
    tiles = pl.pallas_call(
        tiles_kernel,
        out_shape=[jax.ShapeDtypeStruct((16, 128), jnp.float32)] * 8,
        in_specs=[pl.BlockSpec(memory_space=pltpu.SMEM), pl.BlockSpec(memory_space=pltpu.VMEM)],
        out_specs=[pl.BlockSpec(memory_space=pltpu.VMEM)] * 8,
    )(place, matrix)
    return [tiles[0]] + [
        lax.ppermute(tiles[flip], "low", [(i, i ^ flip) for i in range(8)]) for flip in range(1, 8)
    ]


def on_device(
    residual, horiz_vectors, horiz_values, upward_eigen_tables, upward_eigen_values,
    aggregate_map, coarse_inverse,
):
    labels = aggregate_map
    place = lax.axis_index("low").reshape(1)

    parts = call(contributions_kernel, (LINE_SIZE, 2, 128), [labels], [residual])
    sides = (parts, residual[:, :1], residual[:, -1:], coarse_inverse)
    parts, low_side, high_side, matrix = lax.optimization_barrier(sides)
    line_parts = lax.all_to_all(parts, LINE, 0, 0)
    x_low, x_high = neighbours(GROUP, 256, low_side, high_side)
    tiles = regroup(place, matrix)
    line_parts, x_low, x_high, tiles = lax.optimization_barrier((line_parts, x_low, x_high, tiles))

    plane_parts = to_all(line_parts.sum(axis=0), PLANE, PLANE_SIZE)
    plane_parts, x_low, x_high = lax.optimization_barrier((plane_parts, x_low, x_high))
    terms = call(terms_kernel, (LINE_SIZE, 2, 128), [place], [plane_parts] + tiles)
    row_parts = lax.all_to_all(terms, LINE, 0, 0)
    low_side = jnp.concatenate([x_low[:, :, :1], residual[:, :, :1], x_high[:, :, :1]], axis=1)
    high_side = jnp.concatenate([x_low[:, :, -1:], residual[:, :, -1:], x_high[:, :, -1:]], axis=1)
    y_low, y_high = neighbours("high", 4, low_side, high_side)
    local = call(
        local_kernel, residual.shape, [],
        [residual, x_low, x_high, y_low, y_high, horiz_vectors, horiz_values,
         upward_eigen_tables, upward_eigen_values],
        [pltpu.VMEM((POINTS, 512), jnp.float32), pltpu.VMEM((PAIRS, 512), jnp.float32),
         pltpu.VMEM((128, 144), jnp.float32), pltpu.VMEM((1, 144), jnp.float32)],
    )
    row_parts, local = lax.optimization_barrier((row_parts, local))
    coarse = to_all(row_parts.sum(axis=0), PLANE, PLANE_SIZE)
    return call(merge_kernel, residual.shape, [labels], [local, coarse])


def solution(mesh):
    fine = Mesh(mesh.devices.reshape(4, 4, 8, 2, 4), ("y", "x", "low", "core", "high"))
    in_specs = (
        P(None, GROUP, "high", None),
        P(), P(), P(), P(),
        P(GROUP, "high", None),
        P(GROUP, "high"),
    )
    return jax.shard_map(
        on_device, mesh=fine, in_specs=in_specs, out_specs=in_specs[0], check_vma=False
    )
```

```python
import jax
import jax.numpy as jnp
from jax import lax
from jax.experimental import pallas as pl
from jax.experimental.pallas import tpu as pltpu
from jax.sharding import Mesh, PartitionSpec as P

SPAN = 16
EXTENT = 18
WEIGHT = float(SPAN) ** -1.5
PAIRS = 336
POINTS = 336
GROUP = ("y", "x", "low", "core")
PLANE = ("y", "x", "core")
LINE = ("high", "low")
LINE_SIZE = 32
PLANE_SIZE = 32


def iota(shape, dim):
    return lax.broadcasted_iota(jnp.int32, shape, dim)


def split(value):
    high = value.astype(jnp.bfloat16)
    low = (value - high.astype(jnp.float32)).astype(jnp.bfloat16)
    return high, low


def dot3(left, right, dims):
    (lh, ll), (rh, rl) = left, right

    def one(a, b):
        return lax.dot_general(a, b, (dims, ((), ())), preferred_element_type=jnp.float32)

    return one(lh, rh) + (one(lh, rl) + one(ll, rh))


def exact(left, right, dims=((1,), (0,))):
    return lax.dot_general(
        left, right, (dims, ((), ())),
        precision=lax.Precision.HIGHEST, preferred_element_type=jnp.float32,
    )


def point_index(shape, dim):
    row = iota(shape, dim)
    own = row < 256
    plane = row < 288
    far = row >= 312
    x_side = jnp.where(row < 272, 0, EXTENT - 1)
    x = jnp.where(own, (row >> 4) + 1, jnp.where(plane, x_side, row - jnp.where(far, 312, 288)))
    y = jnp.where(own | plane, (row & 15) + 1, jnp.where(far, EXTENT - 1, 0))
    return x, y


def pair_index(shape, dim):
    pair = iota(shape, dim)
    first = (pair * 3641) >> 16
    return first, pair - EXTENT * first


def message_kernel(labels_ref, residual_ref, out_ref):
    lane = iota((1, 128), 1)
    wide = iota((2, 128), 1)
    message = jnp.zeros((1, 128), jnp.float32)
    for j in range(2):
        ys = slice(j * SPAN, (j + 1) * SPAN)
        sums = jnp.concatenate(
            [
                jnp.sum(jnp.sum(residual_ref[v, :, ys, :], axis=0), axis=0, keepdims=True)
                for v in range(2)
            ],
            axis=0,
        )
        for k in range(8):
            total = jnp.sum(jnp.where((wide >> 4) == k, sums, 0.0), axis=1, keepdims=True)
            slot = j * 8 + k
            label = labels_ref[0, j, k].astype(jnp.float32)
            message = jnp.where(lane == slot, total[0:1] * WEIGHT, message)
            message = jnp.where(lane == slot + 16, total[1:2] * WEIGHT, message)
            message = jnp.where(lane == slot + 32, label, message)
    out_ref[...] = jnp.broadcast_to(message[None], out_ref.shape)


def scatter_kernel(slab_ref, parts_ref, out_ref):
    parts = parts_ref[...].reshape(LINE_SIZE, 128)
    lane = iota((LINE_SIZE, 128), 1)
    base = slab_ref[0] * 1024
    first, second, label = (
        [jnp.broadcast_to(parts[:, begin + e : begin + e + 1], parts.shape) for e in range(16)]
        for begin in (0, 16, 32)
    )
    label = [value.astype(jnp.int32) for value in label]
    rows = []
    for values in (first, second):
        for block in range(8):
            column = lane + (base + block * 128)
            total = jnp.zeros_like(parts)
            for e in range(16):
                total = total + jnp.where(label[e] == column, values[e], 0.0)
            rows.append(jnp.sum(total, axis=0, keepdims=True))
    rows = jnp.concatenate(rows, axis=0)
    out_ref[...] = jnp.broadcast_to(rows[None], out_ref.shape)


def terms_kernel(place_ref, parts_ref, matrix_ref, out_ref):
    rhs = jnp.sum(parts_ref[...], axis=0)
    lane = iota((SPAN, 128), 1) - iota((SPAN, 128), 0)
    here = lane == place_ref[0] * SPAN
    terms = []
    for v in range(2):
        total = jnp.zeros((SPAN, 128), jnp.float32)
        for block in range(8):
            row = v * 8 + block
            total = total + matrix_ref[:, block * 128 : (block + 1) * 128] * rhs[row : row + 1]
        column = jnp.sum(total, axis=1, keepdims=True)
        terms.append(jnp.sum(jnp.where(here, column, 0.0), axis=0, keepdims=True))
    terms = jnp.concatenate(terms, axis=0)
    out_ref[...] = jnp.broadcast_to(terms[None], out_ref.shape)


def local_kernel(
    residual_ref, x_low_ref, x_high_ref, y_low_ref, y_high_ref,
    horiz_ref, horiz_values_ref, upward_ref, upward_values_ref,
    out_ref, box_ref, hat_ref, line_ref, line_values_ref,
):
    line_ref[...] = jnp.zeros_like(line_ref)
    for k in range(8):
        begin = 16 * k - 1
        skip = 1 if k == 0 else 0
        stop = 17 if k == 7 else 18
        line_ref[begin + skip : begin + stop, 18 * k : 18 * k + 18] = upward_ref[k, skip:stop, :]
        line_values_ref[0:1, 18 * k : 18 * k + 18] = upward_values_ref[k : k + 1, :]
    line = line_ref[...]
    z = iota((128, 144), 0)
    layer, _ = pair_index((128, 144), 1)
    line_own = split(jnp.where((z >> 4) == layer, line, 0.0))
    line = split(line)

    x_of, y_of = point_index((POINTS, EXTENT), 0)
    mode = iota((POINTS, EXTENT), 1)
    pair_a, pair_b = pair_index((EXTENT, PAIRS), 1)
    table = iota((EXTENT, PAIRS), 0)
    pick_a = jnp.where(pair_a == table, 1.0, 0.0)
    pick_b = jnp.where((pair_b == table) & (pair_a < EXTENT), 1.0, 0.0)
    rows_x = exact(jnp.where(x_of == mode, 1.0, 0.0), exact(horiz_ref[0], pick_a))
    rows_y = exact(jnp.where(y_of == mode, 1.0, 0.0), exact(horiz_ref[1], pick_b))
    plane = split(rows_x * rows_y)
    plane_own = (plane[0][:256], plane[1][:256])

    pair_first, pair_second = pair_index((PAIRS, EXTENT), 0)
    table = iota((PAIRS, EXTENT), 1)
    values = jnp.sum(
        jnp.where(pair_first == table, horiz_values_ref[0:1, :], 0.0)
        + jnp.where(pair_second == table, horiz_values_ref[1:2, :], 0.0),
        axis=1,
        keepdims=True,
    )
    inverse = 1.0 / (values + line_values_ref[...])

    for v in range(2):
        for j in range(2):
            lanes = slice(128 * (2 * v + j), 128 * (2 * v + j + 1))
            ys = slice(j * SPAN, (j + 1) * SPAN)
            box_ref[0:256, lanes] = residual_ref[v, :, ys, :].reshape(256, 128)
            box_ref[256:272, lanes] = x_low_ref[v, 0, ys, :]
            box_ref[272:288, lanes] = x_high_ref[v, 0, ys, :]
            box_ref[304:312, lanes] = jnp.zeros((8, 128), jnp.float32)
            box_ref[328:336, lanes] = jnp.zeros((8, 128), jnp.float32)
            for begin, edge, outer in ((288, 15, y_low_ref), (312, 16, y_high_ref)):
                if (edge == 15) == (j == 0):
                    box_ref[begin : begin + 18, lanes] = outer[v, :, 0, :]
                else:
                    box_ref[begin : begin + 1, lanes] = x_low_ref[v, 0, edge : edge + 1, :]
                    box_ref[begin + 1 : begin + 17, lanes] = residual_ref[v, :, edge, :]
                    box_ref[begin + 17 : begin + 18, lanes] = x_high_ref[v, 0, edge : edge + 1, :]

    hat_ref[...] = dot3(plane, split(box_ref[...]), ((0,), (0,)))
    for part in range(4):
        lanes = slice(128 * part, 128 * (part + 1))
        hat = dot3(split(hat_ref[:, lanes]), line, ((1,), (0,)))
        back = dot3(split(hat * inverse), line_own, ((1,), (1,)))
        solved = dot3(plane_own, split(back), ((1,), (0,)))
        v, j = divmod(part, 2)
        out_ref[v, :, j * SPAN : (j + 1) * SPAN, :] = solved.reshape(SPAN, SPAN, 128)


def merge_kernel(labels_ref, local_ref, coarse_ref, out_ref):
    lane = iota((2, 128), 1)
    for j in range(2):
        update = jnp.zeros((2, 128), jnp.float32)
        for k in range(8):
            label = labels_ref[0, j, k]
            block = ((label >> 8) << 1) | ((label >> 4) & 1)
            place = (((label >> 5) & 7) << 4) | (label & 15)
            value = jnp.sum(
                jnp.where(lane == place, coarse_ref[block], 0.0), axis=1, keepdims=True
            )
            update = update + jnp.where((lane >> 4) == k, value * WEIGHT, 0.0)
        ys = slice(j * SPAN, (j + 1) * SPAN)
        for v in range(2):
            out_ref[v, :, ys, :] = local_ref[v, :, ys, :] + update[v : v + 1][None]


def call(kernel, out_shape, scalars, arrays, scratch=()):
    return pl.pallas_call(
        kernel,
        out_shape=jax.ShapeDtypeStruct(out_shape, jnp.float32),
        in_specs=[pl.BlockSpec(memory_space=pltpu.SMEM)] * len(scalars)
        + [pl.BlockSpec(memory_space=pltpu.VMEM)] * len(arrays),
        out_specs=pl.BlockSpec(memory_space=pltpu.VMEM),
        scratch_shapes=list(scratch),
        compiler_params=pltpu.CompilerParams(vmem_limit_bytes=40 << 20),
    )(*scalars, *arrays)


def to_all(value, axes, size):
    copies = jnp.broadcast_to(value[None], (size,) + value.shape)
    return lax.all_to_all(copies, axes, 0, 0)


def on_device(
    residual, horiz_vectors, horiz_values, upward_eigen_tables, upward_eigen_values,
    aggregate_map, coarse_inverse,
):
    labels = aggregate_map
    place = lax.axis_index("low").reshape(1)
    slab = lax.axis_index("high").reshape(1)
    even = lax.axis_index("core") == 0
    barrier = lax.optimization_barrier

    parts = call(message_kernel, (LINE_SIZE, 1, 128), [labels], [residual])
    first, last = residual[:, :1], residual[:, -1:]
    parts, inner, outer = barrier(
        (parts, jnp.where(even, last, first), jnp.where(even, first, last))
    )
    line_parts = lax.all_to_all(parts, LINE, 0, 0)
    inner = lax.ppermute(inner, GROUP, [(i, i ^ 1) for i in range(256)])
    outer = lax.ppermute(outer, GROUP, [(i, (i + i % 2 * 2 - 1) % 256) for i in range(256)])
    line_parts, inner, outer = barrier((line_parts, inner, outer))
    x_low, x_high = jnp.where(even, outer, inner), jnp.where(even, inner, outer)
    low_side = jnp.concatenate([x_low[:, :, :1], residual[:, :, :1], x_high[:, :, :1]], axis=1)
    high_side = jnp.concatenate([x_low[:, :, -1:], residual[:, :, -1:], x_high[:, :, -1:]], axis=1)

    dense = call(scatter_kernel, (PLANE_SIZE, 16, 128), [slab], [line_parts])
    dense, low_side, high_side = barrier((dense, low_side, high_side))
    plane_parts = lax.all_to_all(dense, PLANE, 0, 0)
    y_low = lax.ppermute(high_side, "high", [(i, (i + 1) % 4) for i in range(4)])
    plane_parts, y_low, low_side = barrier((plane_parts, y_low, low_side))

    terms = call(terms_kernel, (LINE_SIZE, 2, 128), [place], [plane_parts, coarse_inverse])
    terms, low_side = barrier((terms, low_side))
    row_parts = lax.all_to_all(terms, LINE, 0, 0)
    y_high = lax.ppermute(low_side, "high", [(i, (i - 1) % 4) for i in range(4)])
    row_parts, y_high = barrier((row_parts, y_high))
    coarse = to_all(row_parts.sum(axis=0), PLANE, PLANE_SIZE)

    local = call(
        local_kernel, residual.shape, [],
        [residual, x_low, x_high, y_low, y_high, horiz_vectors, horiz_values,
         upward_eigen_tables, upward_eigen_values],
        [pltpu.VMEM((POINTS, 512), jnp.float32), pltpu.VMEM((PAIRS, 512), jnp.float32),
         pltpu.VMEM((128, 144), jnp.float32), pltpu.VMEM((1, 144), jnp.float32)],
    )
    return call(merge_kernel, residual.shape, [labels], [local, coarse])


def solution(mesh):
    fine = Mesh(mesh.devices.reshape(4, 4, 8, 2, 4), ("y", "x", "low", "core", "high"))
    in_specs = (
        P(None, GROUP, "high", None),
        P(), P(), P(), P(),
        P(GROUP, "high", None),
        P(GROUP, "high"),
    )
    return jax.shard_map(
        on_device, mesh=fine, in_specs=in_specs, out_specs=in_specs[0], check_vma=False
    )
```

```python
import jax
import jax.numpy as jnp
from jax import lax
from jax.experimental import pallas as pl
from jax.experimental.pallas import tpu as pltpu
from jax.sharding import Mesh, PartitionSpec as P

SPAN = 16
EXTENT = 18
WEIGHT = float(SPAN) ** -1.5
PAIRS = 336
POINTS = 336
GROUP = ("y", "x", "low", "core")
PLANE = ("y", "x", "core")
LINE = ("high", "low")
LINE_SIZE = 32
LOCAL_FLOPS = 30000000000
PLANE_SIZE = 32


def iota(shape, dim):
    return lax.broadcasted_iota(jnp.int32, shape, dim)


def split(value):
    high = value.astype(jnp.bfloat16)
    low = (value - high.astype(jnp.float32)).astype(jnp.bfloat16)
    return high, low


def dot3(left, right, dims):
    (lh, ll), (rh, rl) = left, right

    def one(a, b):
        return lax.dot_general(a, b, (dims, ((), ())), preferred_element_type=jnp.float32)

    return one(lh, rh) + (one(lh, rl) + one(ll, rh))


def exact(left, right, dims=((1,), (0,))):
    return lax.dot_general(
        left, right, (dims, ((), ())),
        precision=lax.Precision.HIGHEST, preferred_element_type=jnp.float32,
    )


def point_index(shape, dim):
    row = iota(shape, dim)
    own = row < 256
    plane = row < 288
    far = row >= 312
    x_side = jnp.where(row < 272, 0, EXTENT - 1)
    x = jnp.where(own, (row >> 4) + 1, jnp.where(plane, x_side, row - jnp.where(far, 312, 288)))
    y = jnp.where(own | plane, (row & 15) + 1, jnp.where(far, EXTENT - 1, 0))
    return x, y


def pair_index(shape, dim):
    pair = iota(shape, dim)
    first = (pair * 3641) >> 16
    return first, pair - EXTENT * first


def message_kernel(labels_ref, residual_ref, out_ref):
    lane = iota((1, 128), 1)
    wide = iota((2, 128), 1)
    message = jnp.zeros((1, 128), jnp.float32)
    for j in range(2):
        ys = slice(j * SPAN, (j + 1) * SPAN)
        sums = jnp.concatenate(
            [
                jnp.sum(jnp.sum(residual_ref[v, :, ys, :], axis=0), axis=0, keepdims=True)
                for v in range(2)
            ],
            axis=0,
        )
        for k in range(8):
            total = jnp.sum(jnp.where((wide >> 4) == k, sums, 0.0), axis=1, keepdims=True)
            slot = j * 8 + k
            label = labels_ref[0, j, k].astype(jnp.float32)
            message = jnp.where(lane == slot, total[0:1] * WEIGHT, message)
            message = jnp.where(lane == slot + 16, total[1:2] * WEIGHT, message)
            message = jnp.where(lane == slot + 32, label, message)
    out_ref[...] = jnp.broadcast_to(message[None], out_ref.shape)


def scatter_kernel(slab_ref, parts_ref, out_ref):
    parts = parts_ref[...].reshape(LINE_SIZE, 128)
    lane = iota((LINE_SIZE, 128), 1)
    block = (lane & 7) + slab_ref[0] * 8
    values, places = [], []
    for e in range(16):
        first, second, label = (
            jnp.broadcast_to(parts[:, slot : slot + 1], parts.shape) for slot in (e, e + 16, e + 32)
        )
        label = label.astype(jnp.int32)
        here = ((label >> 7) == block) & (lane < 16)
        values.append(jnp.where(here, jnp.where(lane < 8, first, second), 0.0))
        places.append(jnp.where((label & 127) == lane, 1.0, 0.0))
    values = jnp.concatenate(values, axis=0)
    places = jnp.concatenate(places, axis=0)
    rows = exact(values, places, ((0,), (0,)))[:16]
    out_ref[...] = jnp.broadcast_to(rows[None], out_ref.shape)


def terms_kernel(place_ref, parts_ref, matrix_ref, out_ref):
    rhs = jnp.sum(parts_ref[...], axis=0)
    lane = iota((SPAN, 128), 1) - iota((SPAN, 128), 0)
    here = lane == place_ref[0] * SPAN
    terms = []
    for v in range(2):
        total = jnp.zeros((SPAN, 128), jnp.float32)
        for block in range(8):
            row = v * 8 + block
            total = total + matrix_ref[:, block * 128 : (block + 1) * 128] * rhs[row : row + 1]
        column = jnp.sum(total, axis=1, keepdims=True)
        terms.append(jnp.sum(jnp.where(here, column, 0.0), axis=0, keepdims=True))
    terms = jnp.concatenate(terms, axis=0)
    out_ref[...] = jnp.broadcast_to(terms[None], out_ref.shape)


def local_kernel(
    residual_ref, x_low_ref, x_high_ref, y_low_ref, y_high_ref,
    horiz_ref, horiz_values_ref, upward_ref, upward_values_ref,
    out_ref, box_ref, hat_ref, line_ref, line_values_ref,
):
    line_ref[...] = jnp.zeros_like(line_ref)
    for k in range(8):
        begin = 16 * k - 1
        skip = 1 if k == 0 else 0
        stop = 17 if k == 7 else 18
        line_ref[begin + skip : begin + stop, 18 * k : 18 * k + 18] = upward_ref[k, skip:stop, :]
        line_values_ref[0:1, 18 * k : 18 * k + 18] = upward_values_ref[k : k + 1, :]
    line = line_ref[...]
    z = iota((128, 144), 0)
    layer, _ = pair_index((128, 144), 1)
    line_own = split(jnp.where((z >> 4) == layer, line, 0.0))
    line = split(line)

    x_of, y_of = point_index((POINTS, EXTENT), 0)
    mode = iota((POINTS, EXTENT), 1)
    pair_a, pair_b = pair_index((EXTENT, PAIRS), 1)
    table = iota((EXTENT, PAIRS), 0)
    pick_a = jnp.where(pair_a == table, 1.0, 0.0)
    pick_b = jnp.where((pair_b == table) & (pair_a < EXTENT), 1.0, 0.0)
    rows_x = exact(jnp.where(x_of == mode, 1.0, 0.0), exact(horiz_ref[0], pick_a))
    rows_y = exact(jnp.where(y_of == mode, 1.0, 0.0), exact(horiz_ref[1], pick_b))
    plane = split(rows_x * rows_y)
    plane_own = (plane[0][:256], plane[1][:256])

    pair_first, pair_second = pair_index((PAIRS, EXTENT), 0)
    table = iota((PAIRS, EXTENT), 1)
    values = jnp.sum(
        jnp.where(pair_first == table, horiz_values_ref[0:1, :], 0.0)
        + jnp.where(pair_second == table, horiz_values_ref[1:2, :], 0.0),
        axis=1,
        keepdims=True,
    )
    inverse = 1.0 / (values + line_values_ref[...])

    for v in range(2):
        for j in range(2):
            lanes = slice(128 * (2 * v + j), 128 * (2 * v + j + 1))
            ys = slice(j * SPAN, (j + 1) * SPAN)
            box_ref[0:256, lanes] = residual_ref[v, :, ys, :].reshape(256, 128)
            box_ref[256:272, lanes] = x_low_ref[v, 0, ys, :]
            box_ref[272:288, lanes] = x_high_ref[v, 0, ys, :]
            box_ref[304:312, lanes] = jnp.zeros((8, 128), jnp.float32)
            box_ref[328:336, lanes] = jnp.zeros((8, 128), jnp.float32)
            for begin, edge, outer in ((288, 15, y_low_ref), (312, 16, y_high_ref)):
                if (edge == 15) == (j == 0):
                    box_ref[begin : begin + 18, lanes] = outer[v, :, 0, :]
                else:
                    box_ref[begin : begin + 1, lanes] = x_low_ref[v, 0, edge : edge + 1, :]
                    box_ref[begin + 1 : begin + 17, lanes] = residual_ref[v, :, edge, :]
                    box_ref[begin + 17 : begin + 18, lanes] = x_high_ref[v, 0, edge : edge + 1, :]

    hat_ref[...] = dot3(plane, split(box_ref[...]), ((0,), (0,)))
    for part in range(4):
        lanes = slice(128 * part, 128 * (part + 1))
        hat = dot3(split(hat_ref[:, lanes]), line, ((1,), (0,)))
        back = dot3(split(hat * inverse), line_own, ((1,), (1,)))
        solved = dot3(plane_own, split(back), ((1,), (0,)))
        v, j = divmod(part, 2)
        out_ref[v, :, j * SPAN : (j + 1) * SPAN, :] = solved.reshape(SPAN, SPAN, 128)


def merge_kernel(labels_ref, local_ref, coarse_ref, out_ref):
    lane = iota((2, 128), 1)
    for j in range(2):
        update = jnp.zeros((2, 128), jnp.float32)
        for k in range(8):
            label = labels_ref[0, j, k]
            block = ((label >> 8) << 1) | ((label >> 4) & 1)
            place = (((label >> 5) & 7) << 4) | (label & 15)
            value = jnp.sum(
                jnp.where(lane == place, coarse_ref[block], 0.0), axis=1, keepdims=True
            )
            update = update + jnp.where((lane >> 4) == k, value * WEIGHT, 0.0)
        ys = slice(j * SPAN, (j + 1) * SPAN)
        for v in range(2):
            out_ref[v, :, ys, :] = local_ref[v, :, ys, :] + update[v : v + 1][None]


def call(kernel, out_shape, scalars, arrays, scratch=(), cost=None):
    return pl.pallas_call(
        kernel,
        out_shape=jax.ShapeDtypeStruct(out_shape, jnp.float32),
        in_specs=[pl.BlockSpec(memory_space=pltpu.SMEM)] * len(scalars)
        + [pl.BlockSpec(memory_space=pltpu.VMEM)] * len(arrays),
        out_specs=pl.BlockSpec(memory_space=pltpu.VMEM),
        scratch_shapes=list(scratch),
        compiler_params=pltpu.CompilerParams(vmem_limit_bytes=40 << 20),
        cost_estimate=cost,
    )(*scalars, *arrays)


def to_all(value, axes, size):
    copies = jnp.broadcast_to(value[None], (size,) + value.shape)
    return lax.all_to_all(copies, axes, 0, 0)


def on_device(
    residual, horiz_vectors, horiz_values, upward_eigen_tables, upward_eigen_values,
    aggregate_map, coarse_inverse,
):
    labels = aggregate_map
    place = lax.axis_index("low").reshape(1)
    slab = lax.axis_index("high").reshape(1)
    even = lax.axis_index("core") == 0
    barrier = lax.optimization_barrier

    parts = call(message_kernel, (LINE_SIZE, 1, 128), [labels], [residual])
    first, last = residual[:, :1], residual[:, -1:]
    parts, inner, outer = barrier(
        (parts, jnp.where(even, last, first), jnp.where(even, first, last))
    )
    line_parts = lax.all_to_all(parts, LINE, 0, 0)
    inner = lax.ppermute(inner, GROUP, [(i, i ^ 1) for i in range(256)])
    outer = lax.ppermute(outer, GROUP, [(i, (i + i % 2 * 2 - 1) % 256) for i in range(256)])
    line_parts, inner, outer = barrier((line_parts, inner, outer))
    x_low, x_high = jnp.where(even, outer, inner), jnp.where(even, inner, outer)
    low_side = jnp.concatenate([x_low[:, :, :1], residual[:, :, :1], x_high[:, :, :1]], axis=1)
    high_side = jnp.concatenate([x_low[:, :, -1:], residual[:, :, -1:], x_high[:, :, -1:]], axis=1)

    dense = call(scatter_kernel, (PLANE_SIZE, 16, 128), [slab], [line_parts])
    dense, low_side, high_side = barrier((dense, low_side, high_side))
    plane_parts = lax.all_to_all(dense, PLANE, 0, 0)
    plane_parts, low_side, high_side = barrier((plane_parts, low_side, high_side))

    terms = call(terms_kernel, (LINE_SIZE, 2, 128), [place], [plane_parts, coarse_inverse])
    row_parts = lax.all_to_all(terms, LINE, 0, 0)
    y_low = lax.ppermute(high_side, "high", [(i, (i + 1) % 4) for i in range(4)])
    y_high = lax.ppermute(low_side, "high", [(i, (i - 1) % 4) for i in range(4)])
    local = call(
        local_kernel, residual.shape, [],
        [residual, x_low, x_high, y_low, y_high, horiz_vectors, horiz_values,
         upward_eigen_tables, upward_eigen_values],
        [pltpu.VMEM((POINTS, 512), jnp.float32), pltpu.VMEM((PAIRS, 512), jnp.float32),
         pltpu.VMEM((128, 144), jnp.float32), pltpu.VMEM((1, 144), jnp.float32)],
        pl.CostEstimate(flops=LOCAL_FLOPS, transcendentals=0, bytes_accessed=1 << 20),
    )
    row_parts, local = barrier((row_parts, local))
    coarse = to_all(row_parts.sum(axis=0), PLANE, PLANE_SIZE)
    return call(merge_kernel, residual.shape, [labels], [local, coarse])


def solution(mesh):
    fine = Mesh(mesh.devices.reshape(4, 4, 8, 2, 4), ("y", "x", "low", "core", "high"))
    in_specs = (
        P(None, GROUP, "high", None),
        P(), P(), P(), P(),
        P(GROUP, "high", None),
        P(GROUP, "high"),
    )
    return jax.shard_map(
        on_device, mesh=fine, in_specs=in_specs, out_specs=in_specs[0], check_vma=False
    )
```

```python
import jax
import jax.numpy as jnp
from jax import lax
from jax.experimental import pallas as pl
from jax.experimental.pallas import tpu as pltpu
from jax.sharding import Mesh, PartitionSpec as P

SPAN = 16
EXTENT = 18
WEIGHT = float(SPAN) ** -1.5
PAIRS = 336
POINTS = 336
GROUP = ("y", "x", "low", "core")
PLANE = ("y", "x", "core")
LINE = ("high", "low")
LINE_SIZE = 32
PLANE_SIZE = 32


def iota(shape, dim):
    return lax.broadcasted_iota(jnp.int32, shape, dim)


def split(value):
    high = value.astype(jnp.bfloat16)
    low = (value - high.astype(jnp.float32)).astype(jnp.bfloat16)
    return high, low


def dot3(left, right, dims):
    (lh, ll), (rh, rl) = left, right

    def one(a, b):
        return lax.dot_general(a, b, (dims, ((), ())), preferred_element_type=jnp.float32)

    return one(lh, rh) + (one(lh, rl) + one(ll, rh))


def exact(left, right, dims=((1,), (0,))):
    return lax.dot_general(
        left, right, (dims, ((), ())),
        precision=lax.Precision.HIGHEST, preferred_element_type=jnp.float32,
    )


def point_index(shape, dim):
    row = iota(shape, dim)
    own = row < 256
    plane = row < 288
    far = row >= 312
    x_side = jnp.where(row < 272, 0, EXTENT - 1)
    x = jnp.where(own, (row >> 4) + 1, jnp.where(plane, x_side, row - jnp.where(far, 312, 288)))
    y = jnp.where(own | plane, (row & 15) + 1, jnp.where(far, EXTENT - 1, 0))
    return x, y


def pair_index(shape, dim):
    pair = iota(shape, dim)
    first = (pair * 3641) >> 16
    return first, pair - EXTENT * first


def message_kernel(labels_ref, residual_ref, out_ref):
    lane = iota((1, 128), 1)
    wide = iota((2, 128), 1)
    message = jnp.zeros((1, 128), jnp.float32)
    for j in range(2):
        ys = slice(j * SPAN, (j + 1) * SPAN)
        sums = jnp.concatenate(
            [
                jnp.sum(jnp.sum(residual_ref[v, :, ys, :], axis=0), axis=0, keepdims=True)
                for v in range(2)
            ],
            axis=0,
        )
        for k in range(8):
            total = jnp.sum(jnp.where((wide >> 4) == k, sums, 0.0), axis=1, keepdims=True)
            slot = j * 8 + k
            label = labels_ref[0, j, k].astype(jnp.float32)
            message = jnp.where(lane == slot, total[0:1] * WEIGHT, message)
            message = jnp.where(lane == slot + 16, total[1:2] * WEIGHT, message)
            message = jnp.where(lane == slot + 32, label, message)
    out_ref[:, 0:1, :] = jnp.broadcast_to(message[None], (LINE_SIZE, 1, 128))
    out_ref[:, 1, :] = residual_ref[:, :, 2 * SPAN - 1, :].reshape(LINE_SIZE, 128)
    out_ref[:, 2, :] = residual_ref[:, :, 0, :].reshape(LINE_SIZE, 128)


def scatter_kernel(spots_ref, parts_ref, out_ref):
    parts = parts_ref[:, 0, :]
    lane = iota((LINE_SIZE, 128), 1)
    block = (lane & 7) + (spots_ref[0] >> 3) * 8
    values, places = [], []
    for e in range(16):
        first, second, label = (
            jnp.broadcast_to(parts[:, slot : slot + 1], parts.shape) for slot in (e, e + 16, e + 32)
        )
        label = label.astype(jnp.int32)
        here = ((label >> 7) == block) & (lane < 16)
        values.append(jnp.where(here, jnp.where(lane < 8, first, second), 0.0))
        places.append(jnp.where((label & 127) == lane, 1.0, 0.0))
    values = jnp.concatenate(values, axis=0)
    places = jnp.concatenate(places, axis=0)
    rows = exact(values, places, ((0,), (0,)))[:16]
    out_ref[...] = jnp.broadcast_to(rows[None], out_ref.shape)


def terms_kernel(spots_ref, parts_ref, line_ref, x_low_ref, x_high_ref, matrix_ref, out_ref):
    rhs = jnp.sum(parts_ref[...], axis=0)
    lane = iota((SPAN, 128), 1) - iota((SPAN, 128), 0)
    here = lane == (spots_ref[0] & 7) * SPAN
    for v in range(2):
        total = jnp.zeros((SPAN, 128), jnp.float32)
        for block in range(8):
            row = v * 8 + block
            total = total + matrix_ref[:, block * 128 : (block + 1) * 128] * rhs[row : row + 1]
        column = jnp.sum(total, axis=1, keepdims=True)
        terms = jnp.sum(jnp.where(here, column, 0.0), axis=0, keepdims=True)
        out_ref[:, v, :] = jnp.broadcast_to(terms, (LINE_SIZE, 128))
    out_ref[0:8, 2, :] = line_ref[24:32, 1, :]
    out_ref[8:32, 2, :] = line_ref[0:24, 1, :]
    out_ref[0:24, 3, :] = line_ref[8:32, 2, :]
    out_ref[24:32, 3, :] = line_ref[0:8, 2, :]
    out_ref[:, 4:8, :] = jnp.zeros((LINE_SIZE, 4, 128), jnp.float32)
    for spot, edge in ((1, 0), (2, 2 * SPAN - 1)):
        corners = [
            side_ref[v, 0, edge : edge + 1, :] for v in range(2) for side_ref in (x_low_ref, x_high_ref)
        ]
        out_ref[spots_ref[spot], 4:8, :] = jnp.concatenate(corners, axis=0)


def local_kernel(
    spots_ref, residual_ref, x_low_ref, x_high_ref, line_parts_ref,
    horiz_ref, horiz_values_ref, upward_ref, upward_values_ref,
    out_ref, box_ref, hat_ref, line_ref, line_values_ref,
):
    line_ref[...] = jnp.zeros_like(line_ref)
    for k in range(8):
        begin = 16 * k - 1
        skip = 1 if k == 0 else 0
        stop = 17 if k == 7 else 18
        line_ref[begin + skip : begin + stop, 18 * k : 18 * k + 18] = upward_ref[k, skip:stop, :]
        line_values_ref[0:1, 18 * k : 18 * k + 18] = upward_values_ref[k : k + 1, :]
    line = line_ref[...]
    z = iota((128, 144), 0)
    layer, _ = pair_index((128, 144), 1)
    line_own = split(jnp.where((z >> 4) == layer, line, 0.0))
    line = split(line)

    x_of, y_of = point_index((POINTS, EXTENT), 0)
    mode = iota((POINTS, EXTENT), 1)
    pair_a, pair_b = pair_index((EXTENT, PAIRS), 1)
    table = iota((EXTENT, PAIRS), 0)
    pick_a = jnp.where(pair_a == table, 1.0, 0.0)
    pick_b = jnp.where((pair_b == table) & (pair_a < EXTENT), 1.0, 0.0)
    rows_x = exact(jnp.where(x_of == mode, 1.0, 0.0), exact(horiz_ref[0], pick_a))
    rows_y = exact(jnp.where(y_of == mode, 1.0, 0.0), exact(horiz_ref[1], pick_b))
    plane = split(rows_x * rows_y)
    plane_own = (plane[0][:256], plane[1][:256])

    pair_first, pair_second = pair_index((PAIRS, EXTENT), 0)
    table = iota((PAIRS, EXTENT), 1)
    values = jnp.sum(
        jnp.where(pair_first == table, horiz_values_ref[0:1, :], 0.0)
        + jnp.where(pair_second == table, horiz_values_ref[1:2, :], 0.0),
        axis=1,
        keepdims=True,
    )
    inverse = 1.0 / (values + line_values_ref[...])

    for v in range(2):
        for j in range(2):
            lanes = slice(128 * (2 * v + j), 128 * (2 * v + j + 1))
            ys = slice(j * SPAN, (j + 1) * SPAN)
            box_ref[0:256, lanes] = residual_ref[v, :, ys, :].reshape(256, 128)
            box_ref[256:272, lanes] = x_low_ref[v, 0, ys, :]
            box_ref[272:288, lanes] = x_high_ref[v, 0, ys, :]
            box_ref[304:312, lanes] = jnp.zeros((8, 128), jnp.float32)
            box_ref[328:336, lanes] = jnp.zeros((8, 128), jnp.float32)
            for begin, edge, spot in ((288, 15, 1), (312, 16, 2)):
                if (edge == 15) == (j == 0):
                    corner, rows = line_parts_ref[spots_ref[spot]], slice(SPAN * v, SPAN * v + SPAN)
                    box_ref[begin : begin + 1, lanes] = corner[4 + 2 * v : 5 + 2 * v]
                    box_ref[begin + 1 : begin + 17, lanes] = line_parts_ref[rows, spot + 1, :]
                    box_ref[begin + 17 : begin + 18, lanes] = corner[5 + 2 * v : 6 + 2 * v]
                else:
                    box_ref[begin : begin + 1, lanes] = x_low_ref[v, 0, edge : edge + 1, :]
                    box_ref[begin + 1 : begin + 17, lanes] = residual_ref[v, :, edge, :]
                    box_ref[begin + 17 : begin + 18, lanes] = x_high_ref[v, 0, edge : edge + 1, :]

    hat_ref[...] = dot3(plane, split(box_ref[...]), ((0,), (0,)))
    for part in range(4):
        lanes = slice(128 * part, 128 * (part + 1))
        hat = dot3(split(hat_ref[:, lanes]), line, ((1,), (0,)))
        back = dot3(split(hat * inverse), line_own, ((1,), (1,)))
        solved = dot3(plane_own, split(back), ((1,), (0,)))
        v, j = divmod(part, 2)
        out_ref[v, :, j * SPAN : (j + 1) * SPAN, :] = solved.reshape(SPAN, SPAN, 128)


def merge_kernel(labels_ref, local_ref, coarse_ref, out_ref):
    lane = iota((2, 128), 1)
    for j in range(2):
        update = jnp.zeros((2, 128), jnp.float32)
        for k in range(8):
            label = labels_ref[0, j, k]
            block = ((label >> 8) << 1) | ((label >> 4) & 1)
            place = (((label >> 5) & 7) << 4) | (label & 15)
            value = jnp.sum(
                jnp.where(lane == place, coarse_ref[block], 0.0), axis=1, keepdims=True
            )
            update = update + jnp.where((lane >> 4) == k, value * WEIGHT, 0.0)
        ys = slice(j * SPAN, (j + 1) * SPAN)
        for v in range(2):
            out_ref[v, :, ys, :] = local_ref[v, :, ys, :] + update[v : v + 1][None]


def call(kernel, out_shape, scalars, arrays, scratch=()):
    return pl.pallas_call(
        kernel,
        out_shape=jax.ShapeDtypeStruct(out_shape, jnp.float32),
        in_specs=[pl.BlockSpec(memory_space=pltpu.SMEM)] * len(scalars)
        + [pl.BlockSpec(memory_space=pltpu.VMEM)] * len(arrays),
        out_specs=pl.BlockSpec(memory_space=pltpu.VMEM),
        scratch_shapes=list(scratch),
        compiler_params=pltpu.CompilerParams(vmem_limit_bytes=40 << 20),
    )(*scalars, *arrays)


def to_all(value, axes, size):
    copies = jnp.broadcast_to(value[None], (size,) + value.shape)
    return lax.all_to_all(copies, axes, 0, 0)


def on_device(
    residual, horiz_vectors, horiz_values, upward_eigen_tables, upward_eigen_values,
    aggregate_map, coarse_inverse,
):
    labels = aggregate_map
    even = lax.axis_index("core") == 0
    spot = lax.axis_index("high") * 8 + lax.axis_index("low")
    spots = (spot + jnp.array([0, 24, 8], jnp.int32)) % LINE_SIZE
    barrier = lax.optimization_barrier

    parts = call(message_kernel, (LINE_SIZE, 3, 128), [labels], [residual])
    first, last = residual[:, :1], residual[:, -1:]
    parts, inner, outer = barrier(
        (parts, jnp.where(even, last, first), jnp.where(even, first, last))
    )
    line_parts = lax.all_to_all(parts, LINE, 0, 0)
    inner = lax.ppermute(inner, GROUP, [(i, i ^ 1) for i in range(256)])
    outer = lax.ppermute(outer, GROUP, [(i, (i + i % 2 * 2 - 1) % 256) for i in range(256)])
    line_parts, inner, outer = barrier((line_parts, inner, outer))
    x_low, x_high = jnp.where(even, outer, inner), jnp.where(even, inner, outer)

    dense = call(scatter_kernel, (PLANE_SIZE, 16, 128), [spots], [line_parts])
    dense, x_low, x_high = barrier((dense, x_low, x_high))
    plane_parts = lax.all_to_all(dense, PLANE, 0, 0)
    terms = call(
        terms_kernel, (LINE_SIZE, 8, 128), [spots],
        [plane_parts, line_parts, x_low, x_high, coarse_inverse],
    )
    row_parts = lax.all_to_all(terms, LINE, 0, 0)
    coarse = to_all(row_parts[:, :2].sum(axis=0), PLANE, PLANE_SIZE)
    local = call(
        local_kernel, residual.shape, [spots],
        [residual, x_low, x_high, row_parts, horiz_vectors, horiz_values,
         upward_eigen_tables, upward_eigen_values],
        [pltpu.VMEM((POINTS, 512), jnp.float32), pltpu.VMEM((PAIRS, 512), jnp.float32),
         pltpu.VMEM((128, 144), jnp.float32), pltpu.VMEM((1, 144), jnp.float32)],
    )
    return call(merge_kernel, residual.shape, [labels], [local, coarse])


def solution(mesh):
    fine = Mesh(mesh.devices.reshape(4, 4, 8, 2, 4), ("y", "x", "low", "core", "high"))
    in_specs = (
        P(None, GROUP, "high", None),
        P(), P(), P(), P(),
        P(GROUP, "high", None),
        P(GROUP, "high"),
    )
    return jax.shard_map(
        on_device, mesh=fine, in_specs=in_specs, out_specs=in_specs[0], check_vma=False
    )
```

```python
import jax
import jax.numpy as jnp
from jax import lax
from jax.experimental import pallas as pl
from jax.experimental.pallas import tpu as pltpu
from jax.sharding import Mesh, PartitionSpec as P

SPAN = 16
EXTENT = 18
WEIGHT = float(SPAN) ** -1.5
PAIRS = 336
POINTS = 336
GROUP = ("y", "x", "low", "core")
PLANE = ("y", "x", "core")
LINE = ("high", "low")
LINE_SIZE = 32
WINDOW_FLOPS = 1000000000
PLANE_SIZE = 32


def iota(shape, dim):
    return lax.broadcasted_iota(jnp.int32, shape, dim)


def split(value):
    high = value.astype(jnp.bfloat16)
    low = (value - high.astype(jnp.float32)).astype(jnp.bfloat16)
    return high, low


def dot3(left, right, dims):
    (lh, ll), (rh, rl) = left, right

    def one(a, b):
        return lax.dot_general(a, b, (dims, ((), ())), preferred_element_type=jnp.float32)

    return one(lh, rh) + (one(lh, rl) + one(ll, rh))


def exact(left, right, dims=((1,), (0,))):
    return lax.dot_general(
        left, right, (dims, ((), ())),
        precision=lax.Precision.HIGHEST, preferred_element_type=jnp.float32,
    )


def point_index(shape, dim):
    row = iota(shape, dim)
    own = row < 256
    plane = row < 288
    far = row >= 312
    x_side = jnp.where(row < 272, 0, EXTENT - 1)
    x = jnp.where(own, (row >> 4) + 1, jnp.where(plane, x_side, row - jnp.where(far, 312, 288)))
    y = jnp.where(own | plane, (row & 15) + 1, jnp.where(far, EXTENT - 1, 0))
    return x, y


def pair_index(shape, dim):
    pair = iota(shape, dim)
    first = (pair * 3641) >> 16
    return first, pair - EXTENT * first


def message_kernel(labels_ref, residual_ref, out_ref):
    lane = iota((1, 128), 1)
    wide = iota((2, 128), 1)
    message = jnp.zeros((1, 128), jnp.float32)
    for j in range(2):
        ys = slice(j * SPAN, (j + 1) * SPAN)
        sums = jnp.concatenate(
            [
                jnp.sum(jnp.sum(residual_ref[v, :, ys, :], axis=0), axis=0, keepdims=True)
                for v in range(2)
            ],
            axis=0,
        )
        for k in range(8):
            total = jnp.sum(jnp.where((wide >> 4) == k, sums, 0.0), axis=1, keepdims=True)
            slot = j * 8 + k
            label = labels_ref[0, j, k].astype(jnp.float32)
            message = jnp.where(lane == slot, total[0:1] * WEIGHT, message)
            message = jnp.where(lane == slot + 16, total[1:2] * WEIGHT, message)
            message = jnp.where(lane == slot + 32, label, message)
    out_ref[:, 0:1, :] = jnp.broadcast_to(message[None], (LINE_SIZE, 1, 128))
    out_ref[:, 1, :] = residual_ref[:, :, 2 * SPAN - 1, :].reshape(LINE_SIZE, 128)
    out_ref[:, 2, :] = residual_ref[:, :, 0, :].reshape(LINE_SIZE, 128)


def scatter_kernel(spots_ref, parts_ref, out_ref):
    parts = parts_ref[:, 0, :]
    lane = iota((LINE_SIZE, 128), 1)
    block = (lane & 7) + (spots_ref[0] >> 3) * 8
    values, places = [], []
    for e in range(16):
        first, second, label = (
            jnp.broadcast_to(parts[:, slot : slot + 1], parts.shape) for slot in (e, e + 16, e + 32)
        )
        label = label.astype(jnp.int32)
        here = ((label >> 7) == block) & (lane < 16)
        values.append(jnp.where(here, jnp.where(lane < 8, first, second), 0.0))
        places.append(jnp.where((label & 127) == lane, 1.0, 0.0))
    values = jnp.concatenate(values, axis=0)
    places = jnp.concatenate(places, axis=0)
    rows = exact(values, places, ((0,), (0,)))[:16]
    out_ref[...] = jnp.broadcast_to(rows[None], out_ref.shape)


def terms_kernel(spots_ref, parts_ref, line_ref, x_low_ref, x_high_ref, matrix_ref, out_ref):
    rhs = jnp.sum(parts_ref[...], axis=0)
    lane = iota((SPAN, 128), 1) - iota((SPAN, 128), 0)
    here = lane == (spots_ref[0] & 7) * SPAN
    for v in range(2):
        total = jnp.zeros((SPAN, 128), jnp.float32)
        for block in range(8):
            row = v * 8 + block
            total = total + matrix_ref[:, block * 128 : (block + 1) * 128] * rhs[row : row + 1]
        column = jnp.sum(total, axis=1, keepdims=True)
        terms = jnp.sum(jnp.where(here, column, 0.0), axis=0, keepdims=True)
        out_ref[:, v, :] = jnp.broadcast_to(terms, (LINE_SIZE, 128))
    out_ref[0:8, 2, :] = line_ref[24:32, 1, :]
    out_ref[8:32, 2, :] = line_ref[0:24, 1, :]
    out_ref[0:24, 3, :] = line_ref[8:32, 2, :]
    out_ref[24:32, 3, :] = line_ref[0:8, 2, :]
    out_ref[:, 4:8, :] = jnp.zeros((LINE_SIZE, 4, 128), jnp.float32)
    for spot, edge in ((1, 0), (2, 2 * SPAN - 1)):
        corners = [
            side_ref[v, 0, edge : edge + 1, :] for v in range(2) for side_ref in (x_low_ref, x_high_ref)
        ]
        out_ref[spots_ref[spot], 4:8, :] = jnp.concatenate(corners, axis=0)


def prepare_kernel(
    residual_ref, x_low_ref, x_high_ref, horiz_ref, high_ref, low_ref, hat_ref, box_ref
):
    x_of, y_of = point_index((POINTS, EXTENT), 0)
    mode = iota((POINTS, EXTENT), 1)
    pair_a, pair_b = pair_index((EXTENT, PAIRS), 1)
    table = iota((EXTENT, PAIRS), 0)
    pick_a = jnp.where(pair_a == table, 1.0, 0.0)
    pick_b = jnp.where((pair_b == table) & (pair_a < EXTENT), 1.0, 0.0)
    rows_x = exact(jnp.where(x_of == mode, 1.0, 0.0), exact(horiz_ref[0], pick_a))
    rows_y = exact(jnp.where(y_of == mode, 1.0, 0.0), exact(horiz_ref[1], pick_b))
    high, low = split(rows_x * rows_y)
    high_ref[...] = high
    low_ref[...] = low
    for v in range(2):
        for j in range(2):
            lanes = slice(128 * (2 * v + j), 128 * (2 * v + j + 1))
            ys = slice(j * SPAN, (j + 1) * SPAN)
            box_ref[0:256, lanes] = residual_ref[v, :, ys, :].reshape(256, 128)
            box_ref[256:272, lanes] = x_low_ref[v, 0, ys, :]
            box_ref[272:288, lanes] = x_high_ref[v, 0, ys, :]
    hat_ref[...] = dot3((high[:288], low[:288]), split(box_ref[...]), ((0,), (0,)))


def finish_kernel(
    spots_ref, residual_ref, x_low_ref, x_high_ref, line_parts_ref, high_ref, low_ref, hat_ref,
    horiz_values_ref, upward_ref, upward_values_ref,
    out_ref, box_ref, line_ref, line_values_ref,
):
    line_ref[...] = jnp.zeros_like(line_ref)
    for k in range(8):
        begin = 16 * k - 1
        skip = 1 if k == 0 else 0
        stop = 17 if k == 7 else 18
        line_ref[begin + skip : begin + stop, 18 * k : 18 * k + 18] = upward_ref[k, skip:stop, :]
        line_values_ref[0:1, 18 * k : 18 * k + 18] = upward_values_ref[k : k + 1, :]
    line = line_ref[...]
    z = iota((128, 144), 0)
    layer, _ = pair_index((128, 144), 1)
    line_own = split(jnp.where((z >> 4) == layer, line, 0.0))
    line = split(line)

    pair_first, pair_second = pair_index((PAIRS, EXTENT), 0)
    table = iota((PAIRS, EXTENT), 1)
    values = jnp.sum(
        jnp.where(pair_first == table, horiz_values_ref[0:1, :], 0.0)
        + jnp.where(pair_second == table, horiz_values_ref[1:2, :], 0.0),
        axis=1,
        keepdims=True,
    )
    inverse = 1.0 / (values + line_values_ref[...])

    for v in range(2):
        rows = slice(SPAN * v, SPAN * v + SPAN)
        for j in range(2):
            lanes = slice(128 * (2 * v + j), 128 * (2 * v + j + 1))
            for begin, edge, spot in ((0, 15, 1), (24, 16, 2)):
                box_ref[begin + 16 : begin + 24, lanes] = jnp.zeros((8, 128), jnp.float32)
                if (edge == 15) == (j == 0):
                    corner = line_parts_ref[spots_ref[spot]]
                    box_ref[begin : begin + 1, lanes] = corner[4 + 2 * v : 5 + 2 * v]
                    box_ref[begin + 1 : begin + 17, lanes] = line_parts_ref[rows, spot + 1, :]
                    box_ref[begin + 17 : begin + 18, lanes] = corner[5 + 2 * v : 6 + 2 * v]
                else:
                    box_ref[begin : begin + 1, lanes] = x_low_ref[v, 0, edge : edge + 1, :]
                    box_ref[begin + 1 : begin + 17, lanes] = residual_ref[v, :, edge, :]
                    box_ref[begin + 17 : begin + 18, lanes] = x_high_ref[v, 0, edge : edge + 1, :]
    sides = (high_ref[288:336, :], low_ref[288:336, :])
    own = (high_ref[0:256, :], low_ref[0:256, :])
    all_hat = hat_ref[...] + dot3(sides, split(box_ref[...]), ((0,), (0,)))

    for part in range(4):
        hat = dot3(split(all_hat[:, 128 * part : 128 * (part + 1)]), line, ((1,), (0,)))
        back = dot3(split(hat * inverse), line_own, ((1,), (1,)))
        solved = dot3(own, split(back), ((1,), (0,)))
        v, j = divmod(part, 2)
        out_ref[v, :, j * SPAN : (j + 1) * SPAN, :] = solved.reshape(SPAN, SPAN, 128)


def merge_kernel(labels_ref, local_ref, coarse_ref, out_ref):
    lane = iota((2, 128), 1)
    for j in range(2):
        update = jnp.zeros((2, 128), jnp.float32)
        for k in range(8):
            label = labels_ref[0, j, k]
            block = ((label >> 8) << 1) | ((label >> 4) & 1)
            place = (((label >> 5) & 7) << 4) | (label & 15)
            value = jnp.sum(
                jnp.where(lane == place, coarse_ref[block], 0.0), axis=1, keepdims=True
            )
            update = update + jnp.where((lane >> 4) == k, value * WEIGHT, 0.0)
        ys = slice(j * SPAN, (j + 1) * SPAN)
        for v in range(2):
            out_ref[v, :, ys, :] = local_ref[v, :, ys, :] + update[v : v + 1][None]


def call(kernel, out_shape, scalars, arrays, scratch=(), cost=None):
    if not isinstance(out_shape, list):
        out_shape = jax.ShapeDtypeStruct(out_shape, jnp.float32)
    return pl.pallas_call(
        kernel,
        out_shape=out_shape,
        in_specs=[pl.BlockSpec(memory_space=pltpu.SMEM)] * len(scalars)
        + [pl.BlockSpec(memory_space=pltpu.VMEM)] * len(arrays),
        out_specs=jax.tree.map(lambda _: pl.BlockSpec(memory_space=pltpu.VMEM), out_shape),
        scratch_shapes=list(scratch),
        compiler_params=pltpu.CompilerParams(vmem_limit_bytes=40 << 20),
        cost_estimate=cost,
    )(*scalars, *arrays)


def to_all(value, axes, size):
    copies = jnp.broadcast_to(value[None], (size,) + value.shape)
    return lax.all_to_all(copies, axes, 0, 0)


def on_device(
    residual, horiz_vectors, horiz_values, upward_eigen_tables, upward_eigen_values,
    aggregate_map, coarse_inverse,
):
    labels = aggregate_map
    even = lax.axis_index("core") == 0
    spot = lax.axis_index("high") * 8 + lax.axis_index("low")
    spots = (spot + jnp.array([0, 24, 8], jnp.int32)) % LINE_SIZE
    barrier = lax.optimization_barrier

    parts = call(message_kernel, (LINE_SIZE, 3, 128), [labels], [residual])
    first, last = residual[:, :1], residual[:, -1:]
    parts, inner, outer = barrier(
        (parts, jnp.where(even, last, first), jnp.where(even, first, last))
    )
    line_parts = lax.all_to_all(parts, LINE, 0, 0)
    inner = lax.ppermute(inner, GROUP, [(i, i ^ 1) for i in range(256)])
    outer = lax.ppermute(outer, GROUP, [(i, (i + i % 2 * 2 - 1) % 256) for i in range(256)])
    x_low, x_high = jnp.where(even, outer, inner), jnp.where(even, inner, outer)

    dense = call(scatter_kernel, (PLANE_SIZE, 16, 128), [spots], [line_parts])
    plane_parts = lax.all_to_all(dense, PLANE, 0, 0)
    table = jax.ShapeDtypeStruct((POINTS, PAIRS), jnp.bfloat16)
    prepared = call(
        prepare_kernel,
        [table, table, jax.ShapeDtypeStruct((PAIRS, 512), jnp.float32)],
        [], [residual, x_low, x_high, horiz_vectors],
        [pltpu.VMEM((288, 512), jnp.float32)],
        pl.CostEstimate(flops=WINDOW_FLOPS, transcendentals=0, bytes_accessed=1 << 20),
    )
    plane_parts, prepared, x_low, x_high = barrier((plane_parts, prepared, x_low, x_high))
    terms = call(
        terms_kernel, (LINE_SIZE, 8, 128), [spots],
        [plane_parts, line_parts, x_low, x_high, coarse_inverse],
    )
    row_parts = lax.all_to_all(terms, LINE, 0, 0)
    coarse = to_all(row_parts[:, :2].sum(axis=0), PLANE, PLANE_SIZE)
    local = call(
        finish_kernel, residual.shape, [spots],
        [residual, x_low, x_high, row_parts, *prepared, horiz_values,
         upward_eigen_tables, upward_eigen_values],
        [pltpu.VMEM((48, 512), jnp.float32), pltpu.VMEM((128, 144), jnp.float32),
         pltpu.VMEM((1, 144), jnp.float32)],
    )
    return call(merge_kernel, residual.shape, [labels], [local, coarse])


def solution(mesh):
    fine = Mesh(mesh.devices.reshape(4, 4, 8, 2, 4), ("y", "x", "low", "core", "high"))
    in_specs = (
        P(None, GROUP, "high", None),
        P(), P(), P(), P(),
        P(GROUP, "high", None),
        P(GROUP, "high"),
    )
    return jax.shard_map(
        on_device, mesh=fine, in_specs=in_specs, out_specs=in_specs[0], check_vma=False
    )
```

```python
import jax
import jax.numpy as jnp
from jax import lax
from jax.experimental import pallas as pl
from jax.experimental.pallas import tpu as pltpu
from jax.sharding import Mesh, PartitionSpec as P

SPAN = 16
EXTENT = 18
WEIGHT = float(SPAN) ** -1.5
PAIRS = 336
POINTS = 336
GROUP = ("y", "x", "low", "core")
PLANE = ("y", "x", "core")
LINE = ("high", "low")
LINE_SIZE = 32
WINDOW_FLOPS = 1000000000
PLANE_SIZE = 32


def iota(shape, dim):
    return lax.broadcasted_iota(jnp.int32, shape, dim)


def split(value):
    high = value.astype(jnp.bfloat16)
    low = (value - high.astype(jnp.float32)).astype(jnp.bfloat16)
    return high, low


def dot3(left, right, dims):
    (lh, ll), (rh, rl) = left, right

    def one(a, b):
        return lax.dot_general(a, b, (dims, ((), ())), preferred_element_type=jnp.float32)

    return one(lh, rh) + (one(lh, rl) + one(ll, rh))


def exact(left, right, dims=((1,), (0,))):
    return lax.dot_general(
        left, right, (dims, ((), ())),
        precision=lax.Precision.HIGHEST, preferred_element_type=jnp.float32,
    )


def point_index(shape, dim):
    row = iota(shape, dim)
    own = row < 256
    plane = row < 288
    far = row >= 312
    x_side = jnp.where(row < 272, 0, EXTENT - 1)
    x = jnp.where(own, (row >> 4) + 1, jnp.where(plane, x_side, row - jnp.where(far, 312, 288)))
    y = jnp.where(own | plane, (row & 15) + 1, jnp.where(far, EXTENT - 1, 0))
    return x, y


def pair_index(shape, dim):
    pair = iota(shape, dim)
    first = (pair * 3641) >> 16
    return first, pair - EXTENT * first


def message_kernel(
    even_ref, labels_hbm, residual_hbm, out_ref, inner_ref, outer_ref, labels_ref, residual_ref, sems
):
    copies = [pltpu.make_async_copy(residual_hbm.at[v], residual_ref.at[v], sems.at[v]) for v in range(2)]
    copies.append(pltpu.make_async_copy(labels_hbm, labels_ref, sems.at[2]))
    for copy in copies:
        copy.start()
    copies[2].wait()
    lane = iota((1, 128), 1)
    message = jnp.zeros((1, 128), jnp.float32)
    for slot in range(16):
        j, k = divmod(slot, 8)
        label = labels_ref[0, j : j + 1, k : k + 1].astype(jnp.float32)
        message = jnp.where(lane == slot + 32, label, message)
    even = even_ref[0] != 0
    for v in range(2):
        copies[v].wait()
        sums = jnp.concatenate(
            [
                jnp.sum(
                    jnp.sum(residual_ref[v, :, j * SPAN : (j + 1) * SPAN, :], axis=0),
                    axis=0,
                    keepdims=True,
                )
                for j in range(2)
            ],
            axis=0,
        )
        wide = iota((2, 128), 1) >> 4
        for k in range(8):
            total = jnp.sum(jnp.where(wide == k, sums, 0.0), axis=1, keepdims=True)
            for j in range(2):
                slot = v * 16 + j * 8 + k
                message = jnp.where(lane == slot, total[j : j + 1] * WEIGHT, message)
        rows = slice(v * SPAN, (v + 1) * SPAN)
        out_ref[rows, 1, :] = residual_ref[v, :, 2 * SPAN - 1, :]
        out_ref[rows, 2, :] = residual_ref[v, :, 0, :]
        first, last = residual_ref[v, 0], residual_ref[v, SPAN - 1]
        inner_ref[v, 0] = jnp.where(even, last, first)
        outer_ref[v, 0] = jnp.where(even, first, last)
    out_ref[:, 0:1, :] = jnp.broadcast_to(message[None], (LINE_SIZE, 1, 128))


def send_messages(even, labels, residual):
    vectors, _, span_y, span_z = residual.shape
    side = jax.ShapeDtypeStruct((vectors, 1, span_y, span_z), jnp.float32)
    return pl.pallas_call(
        message_kernel,
        out_shape=[jax.ShapeDtypeStruct((LINE_SIZE, 3, 128), jnp.float32), side, side],
        in_specs=[pl.BlockSpec(memory_space=pltpu.SMEM)] + [pl.BlockSpec(memory_space=pl.ANY)] * 2,
        out_specs=[pl.BlockSpec(memory_space=pltpu.VMEM)] * 3,
        scratch_shapes=[
            pltpu.VMEM(labels.shape, jnp.int32),
            pltpu.VMEM(residual.shape, jnp.float32),
            pltpu.SemaphoreType.DMA((3,)),
        ],
    )(even, labels, residual)


def scatter_kernel(spots_ref, parts_ref, out_ref):
    slots = jnp.transpose(parts_ref[:, 0, :])
    slots = jnp.concatenate([slots, jnp.zeros((128, 96), jnp.float32)], axis=1)
    quarter = iota((4, 128), 1) >> 5

    def along_lanes(begin):
        total = slots[begin : begin + 4]
        for q in range(1, 4):
            part = pltpu.roll(slots[begin + 4 * q : begin + 4 * q + 4], 32 * q, 1)
            total = jnp.where(quarter == q, part, total)
        return total

    first, second, label = (along_lanes(begin) for begin in (0, 16, 32))
    label = label.astype(jnp.int32)
    row = iota((SPAN, 128), 0)
    block = (row & 7) + (spots_ref[0] >> 3) * 8
    column = iota((128, 128), 0)
    total = jnp.zeros((SPAN, 128), jnp.float32)
    for g in range(4):
        here = (label[g : g + 1] >> 7) == block
        values = jnp.where(row < 8, first[g : g + 1], second[g : g + 1])
        values = jnp.where(here, values, 0.0)
        places = jnp.where((label[g : g + 1] & 127) == column, 1.0, 0.0)
        total = total + exact(values, places, ((1,), (1,)))
    out_ref[...] = jnp.broadcast_to(total[None], out_ref.shape)


def terms_kernel(spots_ref, parts_ref, line_ref, x_low_ref, x_high_ref, matrix_ref, out_ref):
    rhs = jnp.sum(parts_ref[...], axis=0)
    lane = iota((SPAN, 128), 1) - iota((SPAN, 128), 0)
    here = lane == (spots_ref[0] & 7) * SPAN
    for v in range(2):
        total = jnp.zeros((SPAN, 128), jnp.float32)
        for block in range(8):
            row = v * 8 + block
            total = total + matrix_ref[:, block * 128 : (block + 1) * 128] * rhs[row : row + 1]
        column = jnp.sum(total, axis=1, keepdims=True)
        terms = jnp.sum(jnp.where(here, column, 0.0), axis=0, keepdims=True)
        out_ref[:, v, :] = jnp.broadcast_to(terms, (LINE_SIZE, 128))
    out_ref[0:8, 2, :] = line_ref[24:32, 1, :]
    out_ref[8:32, 2, :] = line_ref[0:24, 1, :]
    out_ref[0:24, 3, :] = line_ref[8:32, 2, :]
    out_ref[24:32, 3, :] = line_ref[0:8, 2, :]
    out_ref[:, 4:8, :] = jnp.zeros((LINE_SIZE, 4, 128), jnp.float32)
    for spot, edge in ((1, 0), (2, 2 * SPAN - 1)):
        corners = [
            side_ref[v, 0, edge : edge + 1, :] for v in range(2) for side_ref in (x_low_ref, x_high_ref)
        ]
        out_ref[spots_ref[spot], 4:8, :] = jnp.concatenate(corners, axis=0)


def prepare_kernel(
    residual_ref, x_low_ref, x_high_ref, horiz_ref, high_ref, low_ref, hat_ref, box_ref
):
    x_of, y_of = point_index((POINTS, EXTENT), 0)
    mode = iota((POINTS, EXTENT), 1)
    pair_a, pair_b = pair_index((EXTENT, PAIRS), 1)
    table = iota((EXTENT, PAIRS), 0)
    pick_a = jnp.where(pair_a == table, 1.0, 0.0)
    pick_b = jnp.where((pair_b == table) & (pair_a < EXTENT), 1.0, 0.0)
    rows_x = exact(jnp.where(x_of == mode, 1.0, 0.0), exact(horiz_ref[0], pick_a))
    rows_y = exact(jnp.where(y_of == mode, 1.0, 0.0), exact(horiz_ref[1], pick_b))
    high, low = split(rows_x * rows_y)
    high_ref[...] = high
    low_ref[...] = low
    for v in range(2):
        for j in range(2):
            lanes = slice(128 * (2 * v + j), 128 * (2 * v + j + 1))
            ys = slice(j * SPAN, (j + 1) * SPAN)
            box_ref[0:256, lanes] = residual_ref[v, :, ys, :].reshape(256, 128)
            box_ref[256:272, lanes] = x_low_ref[v, 0, ys, :]
            box_ref[272:288, lanes] = x_high_ref[v, 0, ys, :]
    hat_ref[...] = dot3((high[:288], low[:288]), split(box_ref[...]), ((0,), (0,)))


def finish_kernel(
    spots_ref, residual_ref, x_low_ref, x_high_ref, line_parts_ref, high_ref, low_ref, hat_ref,
    horiz_values_ref, upward_ref, upward_values_ref,
    out_ref, box_ref, line_ref, line_values_ref,
):
    line_ref[...] = jnp.zeros_like(line_ref)
    for k in range(8):
        begin = 16 * k - 1
        skip = 1 if k == 0 else 0
        stop = 17 if k == 7 else 18
        line_ref[begin + skip : begin + stop, 18 * k : 18 * k + 18] = upward_ref[k, skip:stop, :]
        line_values_ref[0:1, 18 * k : 18 * k + 18] = upward_values_ref[k : k + 1, :]
    line = line_ref[...]
    z = iota((128, 144), 0)
    layer, _ = pair_index((128, 144), 1)
    line_own = split(jnp.where((z >> 4) == layer, line, 0.0))
    line = split(line)

    pair_first, pair_second = pair_index((PAIRS, EXTENT), 0)
    table = iota((PAIRS, EXTENT), 1)
    values = jnp.sum(
        jnp.where(pair_first == table, horiz_values_ref[0:1, :], 0.0)
        + jnp.where(pair_second == table, horiz_values_ref[1:2, :], 0.0),
        axis=1,
        keepdims=True,
    )
    inverse = 1.0 / (values + line_values_ref[...])

    for v in range(2):
        rows = slice(SPAN * v, SPAN * v + SPAN)
        for j in range(2):
            lanes = slice(128 * (2 * v + j), 128 * (2 * v + j + 1))
            for begin, edge, spot in ((0, 15, 1), (24, 16, 2)):
                box_ref[begin + 16 : begin + 24, lanes] = jnp.zeros((8, 128), jnp.float32)
                if (edge == 15) == (j == 0):
                    corner = line_parts_ref[spots_ref[spot]]
                    box_ref[begin : begin + 1, lanes] = corner[4 + 2 * v : 5 + 2 * v]
                    box_ref[begin + 1 : begin + 17, lanes] = line_parts_ref[rows, spot + 1, :]
                    box_ref[begin + 17 : begin + 18, lanes] = corner[5 + 2 * v : 6 + 2 * v]
                else:
                    box_ref[begin : begin + 1, lanes] = x_low_ref[v, 0, edge : edge + 1, :]
                    box_ref[begin + 1 : begin + 17, lanes] = residual_ref[v, :, edge, :]
                    box_ref[begin + 17 : begin + 18, lanes] = x_high_ref[v, 0, edge : edge + 1, :]
    sides = (high_ref[288:336, :], low_ref[288:336, :])
    own = (high_ref[0:256, :], low_ref[0:256, :])
    all_hat = hat_ref[...] + dot3(sides, split(box_ref[...]), ((0,), (0,)))

    for part in range(4):
        hat = dot3(split(all_hat[:, 128 * part : 128 * (part + 1)]), line, ((1,), (0,)))
        back = dot3(split(hat * inverse), line_own, ((1,), (1,)))
        solved = dot3(own, split(back), ((1,), (0,)))
        v, j = divmod(part, 2)
        out_ref[v, :, j * SPAN : (j + 1) * SPAN, :] = solved.reshape(SPAN, SPAN, 128)


def merge_kernel(labels_ref, local_ref, coarse_ref, out_ref):
    lane = iota((2, 128), 1)
    for j in range(2):
        update = jnp.zeros((2, 128), jnp.float32)
        for k in range(8):
            label = labels_ref[0, j, k]
            block = ((label >> 8) << 1) | ((label >> 4) & 1)
            place = (((label >> 5) & 7) << 4) | (label & 15)
            value = jnp.sum(
                jnp.where(lane == place, coarse_ref[block], 0.0), axis=1, keepdims=True
            )
            update = update + jnp.where((lane >> 4) == k, value * WEIGHT, 0.0)
        ys = slice(j * SPAN, (j + 1) * SPAN)
        for v in range(2):
            out_ref[v, :, ys, :] = local_ref[v, :, ys, :] + update[v : v + 1][None]


def call(kernel, out_shape, scalars, arrays, scratch=(), cost=None):
    if not isinstance(out_shape, list):
        out_shape = jax.ShapeDtypeStruct(out_shape, jnp.float32)
    return pl.pallas_call(
        kernel,
        out_shape=out_shape,
        in_specs=[pl.BlockSpec(memory_space=pltpu.SMEM)] * len(scalars)
        + [pl.BlockSpec(memory_space=pltpu.VMEM)] * len(arrays),
        out_specs=jax.tree.map(lambda _: pl.BlockSpec(memory_space=pltpu.VMEM), out_shape),
        scratch_shapes=list(scratch),
        compiler_params=pltpu.CompilerParams(vmem_limit_bytes=40 << 20),
        cost_estimate=cost,
    )(*scalars, *arrays)


def to_all(value, axes, size):
    copies = jnp.broadcast_to(value[None], (size,) + value.shape)
    return lax.all_to_all(copies, axes, 0, 0)


def on_device(
    residual, horiz_vectors, horiz_values, upward_eigen_tables, upward_eigen_values,
    aggregate_map, coarse_inverse,
):
    labels = aggregate_map
    even = lax.axis_index("core") == 0
    spot = lax.axis_index("high") * 8 + lax.axis_index("low")
    spots = (spot + jnp.array([0, 24, 8], jnp.int32)) % LINE_SIZE
    barrier = lax.optimization_barrier

    parts, inner, outer = send_messages(even.astype(jnp.int32).reshape(1), labels, residual)
    parts, inner, outer = barrier((parts, inner, outer))
    line_parts = lax.all_to_all(parts, LINE, 0, 0)
    inner = lax.ppermute(inner, GROUP, [(i, i ^ 1) for i in range(256)])
    outer = lax.ppermute(outer, GROUP, [(i, (i + i % 2 * 2 - 1) % 256) for i in range(256)])
    x_low, x_high = jnp.where(even, outer, inner), jnp.where(even, inner, outer)

    dense = call(scatter_kernel, (PLANE_SIZE, 16, 128), [spots], [line_parts])
    plane_parts = lax.all_to_all(dense, PLANE, 0, 0)
    table = jax.ShapeDtypeStruct((POINTS, PAIRS), jnp.bfloat16)
    prepared = call(
        prepare_kernel,
        [table, table, jax.ShapeDtypeStruct((PAIRS, 512), jnp.float32)],
        [], [residual, x_low, x_high, horiz_vectors],
        [pltpu.VMEM((288, 512), jnp.float32)],
        pl.CostEstimate(flops=WINDOW_FLOPS, transcendentals=0, bytes_accessed=1 << 20),
    )
    plane_parts, prepared, x_low, x_high = barrier((plane_parts, prepared, x_low, x_high))
    terms = call(
        terms_kernel, (LINE_SIZE, 8, 128), [spots],
        [plane_parts, line_parts, x_low, x_high, coarse_inverse],
    )
    row_parts = lax.all_to_all(terms, LINE, 0, 0)
    coarse = to_all(row_parts[:, :2].sum(axis=0), PLANE, PLANE_SIZE)
    local = call(
        finish_kernel, residual.shape, [spots],
        [residual, x_low, x_high, row_parts, *prepared, horiz_values,
         upward_eigen_tables, upward_eigen_values],
        [pltpu.VMEM((48, 512), jnp.float32), pltpu.VMEM((128, 144), jnp.float32),
         pltpu.VMEM((1, 144), jnp.float32)],
    )
    return call(merge_kernel, residual.shape, [labels], [local, coarse])


def solution(mesh):
    fine = Mesh(mesh.devices.reshape(4, 4, 8, 2, 4), ("y", "x", "low", "core", "high"))
    in_specs = (
        P(None, GROUP, "high", None),
        P(), P(), P(), P(),
        P(GROUP, "high", None),
        P(GROUP, "high"),
    )
    return jax.shard_map(
        on_device, mesh=fine, in_specs=in_specs, out_specs=in_specs[0], check_vma=False
    )
```

```python
import jax
import jax.numpy as jnp
from jax import lax
from jax.experimental import pallas as pl
from jax.experimental.pallas import tpu as pltpu
from jax.sharding import Mesh, PartitionSpec as P

SPAN = 16
EXTENT = 18
WEIGHT = float(SPAN) ** -1.5
PAIRS = 336
POINTS = 336
GROUP = ("y", "x", "low", "core")
PLANE = ("y", "x", "core")
LINE = ("high", "low")
LINE_SIZE = 32
WINDOW_FLOPS = 1000000000
PLANE_SIZE = 32


def iota(shape, dim):
    return lax.broadcasted_iota(jnp.int32, shape, dim)


def split(value):
    high = value.astype(jnp.bfloat16)
    low = (value - high.astype(jnp.float32)).astype(jnp.bfloat16)
    return high, low


def dot3(left, right, dims):
    (lh, ll), (rh, rl) = left, right

    def one(a, b):
        return lax.dot_general(a, b, (dims, ((), ())), preferred_element_type=jnp.float32)

    return one(lh, rh) + (one(lh, rl) + one(ll, rh))


def exact(left, right, dims=((1,), (0,))):
    return lax.dot_general(
        left, right, (dims, ((), ())),
        precision=lax.Precision.HIGHEST, preferred_element_type=jnp.float32,
    )


def point_index(shape, dim):
    row = iota(shape, dim)
    own = row < 256
    plane = row < 288
    far = row >= 312
    x_side = jnp.where(row < 272, 0, EXTENT - 1)
    x = jnp.where(own, (row >> 4) + 1, jnp.where(plane, x_side, row - jnp.where(far, 312, 288)))
    y = jnp.where(own | plane, (row & 15) + 1, jnp.where(far, EXTENT - 1, 0))
    return x, y


def pair_index(shape, dim):
    pair = iota(shape, dim)
    first = (pair * 3641) >> 16
    return first, pair - EXTENT * first


def message_kernel(
    even_ref, labels_hbm, residual_hbm, out_ref, inner_ref, outer_ref, labels_ref, residual_ref, sems
):
    copies = [pltpu.make_async_copy(residual_hbm.at[v], residual_ref.at[v], sems.at[v]) for v in range(2)]
    copies.append(pltpu.make_async_copy(labels_hbm, labels_ref, sems.at[2]))
    for copy in copies:
        copy.start()
    copies[2].wait()
    lane = iota((1, 128), 1)
    message = jnp.zeros((1, 128), jnp.float32)
    for slot in range(16):
        j, k = divmod(slot, 8)
        label = labels_ref[0, j : j + 1, k : k + 1].astype(jnp.float32)
        message = jnp.where(lane == slot + 32, label, message)
    even = even_ref[0] != 0
    for v in range(2):
        copies[v].wait()
        sums = jnp.concatenate(
            [
                jnp.sum(
                    jnp.sum(residual_ref[v, :, j * SPAN : (j + 1) * SPAN, :], axis=0),
                    axis=0,
                    keepdims=True,
                )
                for j in range(2)
            ],
            axis=0,
        )
        wide = iota((2, 128), 1) >> 4
        for k in range(8):
            total = jnp.sum(jnp.where(wide == k, sums, 0.0), axis=1, keepdims=True)
            for j in range(2):
                slot = v * 16 + j * 8 + k
                message = jnp.where(lane == slot, total[j : j + 1] * WEIGHT, message)
        rows = slice(v * SPAN, (v + 1) * SPAN)
        out_ref[rows, 0, 128:256] = residual_ref[v, :, 2 * SPAN - 1, :]
        out_ref[rows, 0, 256:384] = residual_ref[v, :, 0, :]
        first, last = residual_ref[v, 0], residual_ref[v, SPAN - 1]
        inner_ref[v, 0] = jnp.where(even, last, first)
        outer_ref[v, 0] = jnp.where(even, first, last)
    out_ref[:, 0, 0:128] = jnp.broadcast_to(message, (LINE_SIZE, 128))


def send_messages(even, labels, residual):
    vectors, _, span_y, span_z = residual.shape
    side = jax.ShapeDtypeStruct((vectors, 1, span_y, span_z), jnp.float32)
    return pl.pallas_call(
        message_kernel,
        out_shape=[jax.ShapeDtypeStruct((LINE_SIZE, 1, 384), jnp.float32), side, side],
        in_specs=[pl.BlockSpec(memory_space=pltpu.SMEM)] + [pl.BlockSpec(memory_space=pl.ANY)] * 2,
        out_specs=[pl.BlockSpec(memory_space=pltpu.VMEM)] * 3,
        scratch_shapes=[
            pltpu.VMEM(labels.shape, jnp.int32),
            pltpu.VMEM(residual.shape, jnp.float32),
            pltpu.SemaphoreType.DMA((3,)),
        ],
    )(even, labels, residual)


def scatter_kernel(spots_ref, parts_ref, out_ref):
    slots = jnp.transpose(parts_ref[:, 0, 0:128])
    slots = jnp.concatenate([slots, jnp.zeros((128, 96), jnp.float32)], axis=1)
    quarter = iota((4, 128), 1) >> 5

    def along_lanes(begin):
        total = slots[begin : begin + 4]
        for q in range(1, 4):
            part = pltpu.roll(slots[begin + 4 * q : begin + 4 * q + 4], 32 * q, 1)
            total = jnp.where(quarter == q, part, total)
        return total

    first, second, label = (along_lanes(begin) for begin in (0, 16, 32))
    label = label.astype(jnp.int32)
    row = iota((SPAN, 128), 0)
    block = (row & 7) + (spots_ref[0] >> 3) * 8
    column = iota((128, 128), 0)
    total = jnp.zeros((SPAN, 128), jnp.float32)
    for g in range(4):
        here = (label[g : g + 1] >> 7) == block
        values = jnp.where(row < 8, first[g : g + 1], second[g : g + 1])
        values = jnp.where(here, values, 0.0)
        places = jnp.where((label[g : g + 1] & 127) == column, 1.0, 0.0)
        total = total + exact(values, places, ((1,), (1,)))
    out_ref[...] = jnp.broadcast_to(total[None], out_ref.shape)


def terms_kernel(spots_ref, parts_ref, line_ref, x_low_ref, x_high_ref, matrix_ref, out_ref):
    rhs = jnp.sum(parts_ref[...], axis=0)
    lane = iota((SPAN, 128), 1) - iota((SPAN, 128), 0)
    place = (spots_ref[0] & 3) * 32
    message = jnp.zeros((1, 128), jnp.float32)
    for v in range(2):
        total = jnp.zeros((SPAN, 128), jnp.float32)
        for block in range(8):
            row = v * 8 + block
            total = total + matrix_ref[:, block * 128 : (block + 1) * 128] * rhs[row : row + 1]
        column = jnp.sum(total, axis=1, keepdims=True)
        here = lane == place + SPAN * v
        message = message + jnp.sum(jnp.where(here, column, 0.0), axis=0, keepdims=True)
    out_ref[:, 0, 0:128] = jnp.broadcast_to(message, (LINE_SIZE, 128))
    out_ref[0:8, 0, 128:256] = line_ref[24:32, 0, 128:256]
    out_ref[8:32, 0, 128:256] = line_ref[0:24, 0, 128:256]
    out_ref[0:24, 0, 256:384] = line_ref[8:32, 0, 256:384]
    out_ref[24:32, 0, 256:384] = line_ref[0:8, 0, 256:384]
    out_ref[:, 0, 384:896] = jnp.zeros((LINE_SIZE, 512), jnp.float32)
    for spot, edge in ((1, 0), (2, 2 * SPAN - 1)):
        corners = [
            side_ref[v, 0, edge : edge + 1, :] for v in range(2) for side_ref in (x_low_ref, x_high_ref)
        ]
        out_ref[spots_ref[spot], :, 384:896] = jnp.concatenate(corners, axis=1)


def prepare_kernel(
    residual_ref, x_low_ref, x_high_ref, horiz_ref, high_ref, low_ref, hat_ref, box_ref
):
    x_of, y_of = point_index((POINTS, EXTENT), 0)
    mode = iota((POINTS, EXTENT), 1)
    pair_a, pair_b = pair_index((EXTENT, PAIRS), 1)
    table = iota((EXTENT, PAIRS), 0)
    pick_a = jnp.where(pair_a == table, 1.0, 0.0)
    pick_b = jnp.where((pair_b == table) & (pair_a < EXTENT), 1.0, 0.0)
    rows_x = exact(jnp.where(x_of == mode, 1.0, 0.0), exact(horiz_ref[0], pick_a))
    rows_y = exact(jnp.where(y_of == mode, 1.0, 0.0), exact(horiz_ref[1], pick_b))
    high, low = split(rows_x * rows_y)
    high_ref[...] = high
    low_ref[...] = low
    for v in range(2):
        for j in range(2):
            lanes = slice(128 * (2 * v + j), 128 * (2 * v + j + 1))
            ys = slice(j * SPAN, (j + 1) * SPAN)
            box_ref[0:256, lanes] = residual_ref[v, :, ys, :].reshape(256, 128)
            box_ref[256:272, lanes] = x_low_ref[v, 0, ys, :]
            box_ref[272:288, lanes] = x_high_ref[v, 0, ys, :]
    hat_ref[...] = dot3((high[:288], low[:288]), split(box_ref[...]), ((0,), (0,)))


def finish_kernel(
    spots_ref, residual_ref, x_low_ref, x_high_ref, line_parts_ref, high_ref, low_ref, hat_ref,
    horiz_values_ref, upward_ref, upward_values_ref,
    out_ref, box_ref, line_ref, line_values_ref,
):
    line_ref[...] = jnp.zeros_like(line_ref)
    for k in range(8):
        begin = 16 * k - 1
        skip = 1 if k == 0 else 0
        stop = 17 if k == 7 else 18
        line_ref[begin + skip : begin + stop, 18 * k : 18 * k + 18] = upward_ref[k, skip:stop, :]
        line_values_ref[0:1, 18 * k : 18 * k + 18] = upward_values_ref[k : k + 1, :]
    line = line_ref[...]
    z = iota((128, 144), 0)
    layer, _ = pair_index((128, 144), 1)
    line_own = split(jnp.where((z >> 4) == layer, line, 0.0))
    line = split(line)

    pair_first, pair_second = pair_index((PAIRS, EXTENT), 0)
    table = iota((PAIRS, EXTENT), 1)
    values = jnp.sum(
        jnp.where(pair_first == table, horiz_values_ref[0:1, :], 0.0)
        + jnp.where(pair_second == table, horiz_values_ref[1:2, :], 0.0),
        axis=1,
        keepdims=True,
    )
    inverse = 1.0 / (values + line_values_ref[...])

    for v in range(2):
        rows = slice(SPAN * v, SPAN * v + SPAN)
        for j in range(2):
            lanes = slice(128 * (2 * v + j), 128 * (2 * v + j + 1))
            for begin, edge, spot in ((0, 15, 1), (24, 16, 2)):
                box_ref[begin + 16 : begin + 24, lanes] = jnp.zeros((8, 128), jnp.float32)
                if (edge == 15) == (j == 0):
                    corner = line_parts_ref[spots_ref[spot]]
                    first = 128 * (3 + 2 * v)
                    side = slice(128 * spot, 128 * (spot + 1))
                    box_ref[begin : begin + 1, lanes] = corner[:, first : first + 128]
                    box_ref[begin + 1 : begin + 17, lanes] = line_parts_ref[rows, 0, side]
                    box_ref[begin + 17 : begin + 18, lanes] = corner[:, first + 128 : first + 256]
                else:
                    box_ref[begin : begin + 1, lanes] = x_low_ref[v, 0, edge : edge + 1, :]
                    box_ref[begin + 1 : begin + 17, lanes] = residual_ref[v, :, edge, :]
                    box_ref[begin + 17 : begin + 18, lanes] = x_high_ref[v, 0, edge : edge + 1, :]
    sides = (high_ref[288:336, :], low_ref[288:336, :])
    own = (high_ref[0:256, :], low_ref[0:256, :])
    all_hat = hat_ref[...] + dot3(sides, split(box_ref[...]), ((0,), (0,)))

    for part in range(4):
        hat = dot3(split(all_hat[:, 128 * part : 128 * (part + 1)]), line, ((1,), (0,)))
        back = dot3(split(hat * inverse), line_own, ((1,), (1,)))
        solved = dot3(own, split(back), ((1,), (0,)))
        v, j = divmod(part, 2)
        out_ref[v, :, j * SPAN : (j + 1) * SPAN, :] = solved.reshape(SPAN, SPAN, 128)


def merge_kernel(labels_ref, local_ref, coarse_ref, out_ref):
    lane = iota((1, 128), 1)
    for j in range(2):
        updates = [jnp.zeros((1, 128), jnp.float32)] * 2
        for k in range(8):
            label = labels_ref[0, j, k]
            block = ((label >> 8) << 1) | ((label >> 4) & 1)
            place = (((label >> 5) & 3) << 5) | (label & 15)
            row = coarse_ref[block, pl.ds((label >> 7) & 1, 1), :]
            for v in range(2):
                here = lane == place + SPAN * v
                value = jnp.sum(jnp.where(here, row, 0.0), axis=1, keepdims=True)
                updates[v] = jnp.where((lane >> 4) == k, value * WEIGHT, updates[v])
        ys = slice(j * SPAN, (j + 1) * SPAN)
        for v in range(2):
            out_ref[v, :, ys, :] = local_ref[v, :, ys, :] + updates[v][None]


def call(kernel, out_shape, scalars, arrays, scratch=(), cost=None):
    if not isinstance(out_shape, list):
        out_shape = jax.ShapeDtypeStruct(out_shape, jnp.float32)
    return pl.pallas_call(
        kernel,
        out_shape=out_shape,
        in_specs=[pl.BlockSpec(memory_space=pltpu.SMEM)] * len(scalars)
        + [pl.BlockSpec(memory_space=pltpu.VMEM)] * len(arrays),
        out_specs=jax.tree.map(lambda _: pl.BlockSpec(memory_space=pltpu.VMEM), out_shape),
        scratch_shapes=list(scratch),
        compiler_params=pltpu.CompilerParams(vmem_limit_bytes=40 << 20),
        cost_estimate=cost,
    )(*scalars, *arrays)


def to_all(value, axes, size):
    copies = jnp.broadcast_to(value[None], (size,) + value.shape)
    return lax.all_to_all(copies, axes, 0, 0)


def on_device(
    residual, horiz_vectors, horiz_values, upward_eigen_tables, upward_eigen_values,
    aggregate_map, coarse_inverse,
):
    labels = aggregate_map
    even = lax.axis_index("core") == 0
    spot = lax.axis_index("high") * 8 + lax.axis_index("low")
    spots = (spot + jnp.array([0, 24, 8], jnp.int32)) % LINE_SIZE
    barrier = lax.optimization_barrier

    parts, inner, outer = send_messages(even.astype(jnp.int32).reshape(1), labels, residual)
    parts, inner, outer = barrier((parts, inner, outer))
    line_parts = lax.all_to_all(parts, LINE, 0, 0)
    inner = lax.ppermute(inner, GROUP, [(i, i ^ 1) for i in range(256)])
    outer = lax.ppermute(outer, GROUP, [(i, (i + i % 2 * 2 - 1) % 256) for i in range(256)])
    x_low, x_high = jnp.where(even, outer, inner), jnp.where(even, inner, outer)

    dense = call(scatter_kernel, (PLANE_SIZE, 16, 128), [spots], [line_parts])
    plane_parts = lax.all_to_all(dense, PLANE, 0, 0)
    table = jax.ShapeDtypeStruct((POINTS, PAIRS), jnp.bfloat16)
    prepared = call(
        prepare_kernel,
        [table, table, jax.ShapeDtypeStruct((PAIRS, 512), jnp.float32)],
        [], [residual, x_low, x_high, horiz_vectors],
        [pltpu.VMEM((288, 512), jnp.float32)],
        pl.CostEstimate(flops=WINDOW_FLOPS, transcendentals=0, bytes_accessed=1 << 20),
    )
    plane_parts, prepared, x_low, x_high = barrier((plane_parts, prepared, x_low, x_high))
    terms = call(
        terms_kernel, (LINE_SIZE, 1, 896), [spots],
        [plane_parts, line_parts, x_low, x_high, coarse_inverse],
    )
    row_parts = lax.all_to_all(terms, LINE, 0, 0)
    rows = row_parts[:, 0, :128].reshape(4, 2, 4, 128).sum(axis=(0, 2))
    coarse = to_all(rows, PLANE, PLANE_SIZE)
    local = call(
        finish_kernel, residual.shape, [spots],
        [residual, x_low, x_high, row_parts, *prepared, horiz_values,
         upward_eigen_tables, upward_eigen_values],
        [pltpu.VMEM((48, 512), jnp.float32), pltpu.VMEM((128, 144), jnp.float32),
         pltpu.VMEM((1, 144), jnp.float32)],
    )
    return call(merge_kernel, residual.shape, [labels], [local, coarse])


def solution(mesh):
    fine = Mesh(mesh.devices.reshape(4, 4, 8, 2, 4), ("y", "x", "low", "core", "high"))
    in_specs = (
        P(None, GROUP, "high", None),
        P(), P(), P(), P(),
        P(GROUP, "high", None),
        P(GROUP, "high"),
    )
    return jax.shard_map(
        on_device, mesh=fine, in_specs=in_specs, out_specs=in_specs[0], check_vma=False
    )
```

```python
import jax
import jax.numpy as jnp
from jax import lax
from jax.experimental import pallas as pl
from jax.experimental.pallas import tpu as pltpu
from jax.sharding import Mesh, PartitionSpec as P

SPAN = 16
EXTENT = 18
WEIGHT = float(SPAN) ** -1.5
PAIRS = 336
POINTS = 336
GROUP = ("y", "x", "low", "core")
PLANE = ("y", "x", "core")
LINE = ("high", "low")
LINE_SIZE = 32
WINDOW_FLOPS = 1000000000
PLANE_SIZE = 32


def iota(shape, dim):
    return lax.broadcasted_iota(jnp.int32, shape, dim)


def split(value):
    high = value.astype(jnp.bfloat16)
    low = (value - high.astype(jnp.float32)).astype(jnp.bfloat16)
    return high, low


def dot3(left, right, dims):
    (lh, ll), (rh, rl) = left, right

    def one(a, b):
        return lax.dot_general(a, b, (dims, ((), ())), preferred_element_type=jnp.float32)

    return one(lh, rh) + (one(lh, rl) + one(ll, rh))


def exact(left, right, dims=((1,), (0,))):
    return lax.dot_general(
        left, right, (dims, ((), ())),
        precision=lax.Precision.HIGHEST, preferred_element_type=jnp.float32,
    )


def point_index(shape, dim):
    row = iota(shape, dim)
    own = row < 256
    plane = row < 288
    far = row >= 312
    x_side = jnp.where(row < 272, 0, EXTENT - 1)
    x = jnp.where(own, (row >> 4) + 1, jnp.where(plane, x_side, row - jnp.where(far, 312, 288)))
    y = jnp.where(own | plane, (row & 15) + 1, jnp.where(far, EXTENT - 1, 0))
    return x, y


def pair_index(shape, dim):
    pair = iota(shape, dim)
    first = (pair * 3641) >> 16
    return first, pair - EXTENT * first


def message_kernel(
    even_ref, labels_hbm, residual_hbm, out_ref, inner_ref, outer_ref, labels_ref, residual_ref, sems
):
    copies = [pltpu.make_async_copy(residual_hbm.at[v], residual_ref.at[v], sems.at[v]) for v in range(2)]
    copies.append(pltpu.make_async_copy(labels_hbm, labels_ref, sems.at[2]))
    for copy in copies:
        copy.start()
    copies[2].wait()
    lane = iota((1, 128), 1)
    message = jnp.zeros((1, 128), jnp.float32)
    for slot in range(16):
        j, k = divmod(slot, 8)
        label = labels_ref[0, j : j + 1, k : k + 1].astype(jnp.float32)
        message = jnp.where(lane == slot + 32, label, message)
    even = even_ref[0] != 0
    for v in range(2):
        copies[v].wait()
        sums = jnp.concatenate(
            [
                jnp.sum(
                    jnp.sum(residual_ref[v, :, j * SPAN : (j + 1) * SPAN, :], axis=0),
                    axis=0,
                    keepdims=True,
                )
                for j in range(2)
            ],
            axis=0,
        )
        wide = iota((2, 128), 1) >> 4
        for k in range(8):
            total = jnp.sum(jnp.where(wide == k, sums, 0.0), axis=1, keepdims=True)
            for j in range(2):
                slot = v * 16 + j * 8 + k
                message = jnp.where(lane == slot, total[j : j + 1] * WEIGHT, message)
        rows = slice(v * SPAN, (v + 1) * SPAN)
        out_ref[rows, 0, 128:256] = residual_ref[v, :, 2 * SPAN - 1, :]
        out_ref[rows, 0, 256:384] = residual_ref[v, :, 0, :]
        first, last = residual_ref[v, 0], residual_ref[v, SPAN - 1]
        inner_ref[v, 0] = jnp.where(even, last, first)
        outer_ref[v, 0] = jnp.where(even, first, last)
    out_ref[:, 0, 0:128] = jnp.broadcast_to(message, (LINE_SIZE, 128))


def send_messages(even, labels, residual):
    vectors, _, span_y, span_z = residual.shape
    side = jax.ShapeDtypeStruct((vectors, 1, span_y, span_z), jnp.float32)
    return pl.pallas_call(
        message_kernel,
        out_shape=[jax.ShapeDtypeStruct((LINE_SIZE, 1, 384), jnp.float32), side, side],
        in_specs=[pl.BlockSpec(memory_space=pltpu.SMEM)] + [pl.BlockSpec(memory_space=pl.ANY)] * 2,
        out_specs=[pl.BlockSpec(memory_space=pltpu.VMEM)] * 3,
        scratch_shapes=[
            pltpu.VMEM(labels.shape, jnp.int32),
            pltpu.VMEM(residual.shape, jnp.float32),
            pltpu.SemaphoreType.DMA((3,)),
        ],
    )(even, labels, residual)


def scatter_kernel(spots_ref, parts_ref, out_ref):
    slots = jnp.transpose(parts_ref[:, 0, 0:128])
    slots = jnp.concatenate([slots, jnp.zeros((128, 96), jnp.float32)], axis=1)
    quarter = iota((4, 128), 1) >> 5

    def along_lanes(begin):
        total = slots[begin : begin + 4]
        for q in range(1, 4):
            part = pltpu.roll(slots[begin + 4 * q : begin + 4 * q + 4], 32 * q, 1)
            total = jnp.where(quarter == q, part, total)
        return total

    first, second, label = (along_lanes(begin) for begin in (0, 16, 32))
    label = label.astype(jnp.int32)
    row = iota((SPAN, 128), 0)
    block = (row & 7) + (spots_ref[0] >> 3) * 8
    column = iota((128, 128), 0)
    total = jnp.zeros((SPAN, 128), jnp.float32)
    for g in range(4):
        here = (label[g : g + 1] >> 7) == block
        values = jnp.where(row < 8, first[g : g + 1], second[g : g + 1])
        values = jnp.where(here, values, 0.0)
        places = jnp.where((label[g : g + 1] & 127) == column, 1.0, 0.0)
        total = total + exact(values, places, ((1,), (1,)))
    out_ref[...] = jnp.broadcast_to(total[None], out_ref.shape)


def terms_kernel(spots_ref, parts_ref, line_ref, x_low_ref, x_high_ref, matrix_ref, out_ref):
    rhs = jnp.sum(parts_ref[...], axis=0)
    lane = iota((SPAN, 128), 1) - iota((SPAN, 128), 0)
    place = (spots_ref[0] & 3) * 32
    message = jnp.zeros((1, 128), jnp.float32)
    for v in range(2):
        total = jnp.zeros((SPAN, 128), jnp.float32)
        for block in range(8):
            row = v * 8 + block
            total = total + matrix_ref[:, block * 128 : (block + 1) * 128] * rhs[row : row + 1]
        column = jnp.sum(total, axis=1, keepdims=True)
        here = lane == place + SPAN * v
        message = message + jnp.sum(jnp.where(here, column, 0.0), axis=0, keepdims=True)
    out_ref[:, 0, 0:128] = jnp.broadcast_to(message, (LINE_SIZE, 128))
    out_ref[0:8, 0, 128:256] = line_ref[24:32, 0, 128:256]
    out_ref[8:32, 0, 128:256] = line_ref[0:24, 0, 128:256]
    out_ref[0:24, 0, 256:384] = line_ref[8:32, 0, 256:384]
    out_ref[24:32, 0, 256:384] = line_ref[0:8, 0, 256:384]
    out_ref[:, 0, 384:896] = jnp.zeros((LINE_SIZE, 512), jnp.float32)
    for spot, edge in ((1, 0), (2, 2 * SPAN - 1)):
        corners = [
            side_ref[v, 0, edge : edge + 1, :] for v in range(2) for side_ref in (x_low_ref, x_high_ref)
        ]
        out_ref[spots_ref[spot], :, 384:896] = jnp.concatenate(corners, axis=1)


def prepare_kernel(
    residual_ref, x_low_ref, x_high_ref, horiz_ref, horiz_values_ref, upward_ref, upward_values_ref,
    high_ref, low_ref, hat_ref, line_high_ref, line_low_ref, own_high_ref, own_low_ref, inverse_ref,
    box_ref, line_ref, line_values_ref,
):
    x_of, y_of = point_index((POINTS, EXTENT), 0)
    mode = iota((POINTS, EXTENT), 1)
    pair_a, pair_b = pair_index((EXTENT, PAIRS), 1)
    table = iota((EXTENT, PAIRS), 0)
    pick_a = jnp.where(pair_a == table, 1.0, 0.0)
    pick_b = jnp.where((pair_b == table) & (pair_a < EXTENT), 1.0, 0.0)
    rows_x = exact(jnp.where(x_of == mode, 1.0, 0.0), exact(horiz_ref[0], pick_a))
    rows_y = exact(jnp.where(y_of == mode, 1.0, 0.0), exact(horiz_ref[1], pick_b))
    high, low = split(rows_x * rows_y)
    high_ref[...] = high
    low_ref[...] = low
    for v in range(2):
        for j in range(2):
            lanes = slice(128 * (2 * v + j), 128 * (2 * v + j + 1))
            ys = slice(j * SPAN, (j + 1) * SPAN)
            box_ref[0:256, lanes] = residual_ref[v, :, ys, :].reshape(256, 128)
            box_ref[256:272, lanes] = x_low_ref[v, 0, ys, :]
            box_ref[272:288, lanes] = x_high_ref[v, 0, ys, :]
    hat_ref[...] = dot3((high[:288], low[:288]), split(box_ref[...]), ((0,), (0,)))

    line_ref[...] = jnp.zeros_like(line_ref)
    for k in range(8):
        begin = 16 * k - 1
        skip = 1 if k == 0 else 0
        stop = 17 if k == 7 else 18
        line_ref[begin + skip : begin + stop, 18 * k : 18 * k + 18] = upward_ref[k, skip:stop, :]
        line_values_ref[0:1, 18 * k : 18 * k + 18] = upward_values_ref[k : k + 1, :]
    line = line_ref[...]
    z = iota((128, 144), 0)
    layer, _ = pair_index((128, 144), 1)
    line_high_ref[...], line_low_ref[...] = split(line)
    own_high_ref[...], own_low_ref[...] = split(jnp.where((z >> 4) == layer, line, 0.0))

    pair_first, pair_second = pair_index((PAIRS, EXTENT), 0)
    table = iota((PAIRS, EXTENT), 1)
    values = jnp.sum(
        jnp.where(pair_first == table, horiz_values_ref[0:1, :], 0.0)
        + jnp.where(pair_second == table, horiz_values_ref[1:2, :], 0.0),
        axis=1,
        keepdims=True,
    )
    inverse_ref[...] = 1.0 / (values + line_values_ref[...])


def finish_kernel(
    spots_ref, residual_ref, x_low_ref, x_high_ref, line_parts_ref, high_ref, low_ref, hat_ref,
    line_high_ref, line_low_ref, own_high_ref, own_low_ref, inverse_ref, out_ref, box_ref,
):
    for v in range(2):
        rows = slice(SPAN * v, SPAN * v + SPAN)
        for j in range(2):
            lanes = slice(128 * (2 * v + j), 128 * (2 * v + j + 1))
            for begin, edge, spot in ((0, 15, 1), (24, 16, 2)):
                box_ref[begin + 16 : begin + 24, lanes] = jnp.zeros((8, 128), jnp.float32)
                if (edge == 15) == (j == 0):
                    corner = line_parts_ref[spots_ref[spot]]
                    first = 128 * (3 + 2 * v)
                    side = slice(128 * spot, 128 * (spot + 1))
                    box_ref[begin : begin + 1, lanes] = corner[:, first : first + 128]
                    box_ref[begin + 1 : begin + 17, lanes] = line_parts_ref[rows, 0, side]
                    box_ref[begin + 17 : begin + 18, lanes] = corner[:, first + 128 : first + 256]
                else:
                    box_ref[begin : begin + 1, lanes] = x_low_ref[v, 0, edge : edge + 1, :]
                    box_ref[begin + 1 : begin + 17, lanes] = residual_ref[v, :, edge, :]
                    box_ref[begin + 17 : begin + 18, lanes] = x_high_ref[v, 0, edge : edge + 1, :]
    sides = (high_ref[288:336, :], low_ref[288:336, :])
    own = (high_ref[0:256, :], low_ref[0:256, :])
    line = (line_high_ref[...], line_low_ref[...])
    line_own = (own_high_ref[...], own_low_ref[...])
    inverse = inverse_ref[...]
    all_hat = hat_ref[...] + dot3(sides, split(box_ref[...]), ((0,), (0,)))

    for part in range(4):
        hat = dot3(split(all_hat[:, 128 * part : 128 * (part + 1)]), line, ((1,), (0,)))
        back = dot3(split(hat * inverse), line_own, ((1,), (1,)))
        solved = dot3(own, split(back), ((1,), (0,)))
        v, j = divmod(part, 2)
        out_ref[v, :, j * SPAN : (j + 1) * SPAN, :] = solved.reshape(SPAN, SPAN, 128)


def merge_kernel(labels_ref, local_ref, coarse_ref, out_ref):
    lane = iota((1, 128), 1)
    for j in range(2):
        updates = [jnp.zeros((1, 128), jnp.float32)] * 2
        for k in range(8):
            label = labels_ref[0, j, k]
            block = ((label >> 8) << 1) | ((label >> 4) & 1)
            place = (((label >> 5) & 3) << 5) | (label & 15)
            row = coarse_ref[block, pl.ds((label >> 7) & 1, 1), :]
            for v in range(2):
                here = lane == place + SPAN * v
                value = jnp.sum(jnp.where(here, row, 0.0), axis=1, keepdims=True)
                updates[v] = jnp.where((lane >> 4) == k, value * WEIGHT, updates[v])
        ys = slice(j * SPAN, (j + 1) * SPAN)
        for v in range(2):
            out_ref[v, :, ys, :] = local_ref[v, :, ys, :] + updates[v][None]


def call(kernel, out_shape, scalars, arrays, scratch=(), cost=None):
    if not isinstance(out_shape, list):
        out_shape = jax.ShapeDtypeStruct(out_shape, jnp.float32)
    return pl.pallas_call(
        kernel,
        out_shape=out_shape,
        in_specs=[pl.BlockSpec(memory_space=pltpu.SMEM)] * len(scalars)
        + [pl.BlockSpec(memory_space=pltpu.VMEM)] * len(arrays),
        out_specs=jax.tree.map(lambda _: pl.BlockSpec(memory_space=pltpu.VMEM), out_shape),
        scratch_shapes=list(scratch),
        compiler_params=pltpu.CompilerParams(vmem_limit_bytes=40 << 20),
        cost_estimate=cost,
    )(*scalars, *arrays)


def to_all(value, axes, size):
    copies = jnp.broadcast_to(value[None], (size,) + value.shape)
    return lax.all_to_all(copies, axes, 0, 0)


def on_device(
    residual, horiz_vectors, horiz_values, upward_eigen_tables, upward_eigen_values,
    aggregate_map, coarse_inverse,
):
    labels = aggregate_map
    even = lax.axis_index("core") == 0
    spot = lax.axis_index("high") * 8 + lax.axis_index("low")
    spots = (spot + jnp.array([0, 24, 8], jnp.int32)) % LINE_SIZE
    barrier = lax.optimization_barrier

    parts, inner, outer = send_messages(even.astype(jnp.int32).reshape(1), labels, residual)
    parts, inner, outer = barrier((parts, inner, outer))
    line_parts = lax.all_to_all(parts, LINE, 0, 0)
    inner = lax.ppermute(inner, GROUP, [(i, i ^ 1) for i in range(256)])
    outer = lax.ppermute(outer, GROUP, [(i, (i + i % 2 * 2 - 1) % 256) for i in range(256)])
    x_low, x_high = jnp.where(even, outer, inner), jnp.where(even, inner, outer)

    dense = call(scatter_kernel, (PLANE_SIZE, 16, 128), [spots], [line_parts])
    plane_parts = lax.all_to_all(dense, PLANE, 0, 0)
    table = jax.ShapeDtypeStruct((POINTS, PAIRS), jnp.bfloat16)
    line_table = jax.ShapeDtypeStruct((128, 144), jnp.bfloat16)
    sums, reciprocals = (jax.ShapeDtypeStruct((PAIRS, n), jnp.float32) for n in (512, 144))
    prepared = call(
        prepare_kernel,
        [table, table, sums, line_table, line_table, line_table, line_table, reciprocals],
        [],
        [residual, x_low, x_high, horiz_vectors, horiz_values, upward_eigen_tables, upward_eigen_values],
        [pltpu.VMEM((288, 512), jnp.float32), pltpu.VMEM((128, 144), jnp.float32),
         pltpu.VMEM((1, 144), jnp.float32)],
        pl.CostEstimate(flops=WINDOW_FLOPS, transcendentals=0, bytes_accessed=1 << 20),
    )
    plane_parts, prepared, x_low, x_high = barrier((plane_parts, prepared, x_low, x_high))
    terms = call(
        terms_kernel, (LINE_SIZE, 1, 896), [spots],
        [plane_parts, line_parts, x_low, x_high, coarse_inverse],
    )
    row_parts = lax.all_to_all(terms, LINE, 0, 0)
    rows = row_parts[:, 0, :128].reshape(4, 2, 4, 128).sum(axis=(0, 2))
    coarse = to_all(rows, PLANE, PLANE_SIZE)
    local = call(
        finish_kernel, residual.shape, [spots],
        [residual, x_low, x_high, row_parts, *prepared],
        [pltpu.VMEM((48, 512), jnp.float32)],
    )
    return call(merge_kernel, residual.shape, [labels], [local, coarse])


def solution(mesh):
    fine = Mesh(mesh.devices.reshape(4, 4, 8, 2, 4), ("y", "x", "low", "core", "high"))
    in_specs = (
        P(None, GROUP, "high", None),
        P(), P(), P(), P(),
        P(GROUP, "high", None),
        P(GROUP, "high"),
    )
    return jax.shard_map(
        on_device, mesh=fine, in_specs=in_specs, out_specs=in_specs[0], check_vma=False
    )
```

```python
import jax
import jax.numpy as jnp
from jax import lax
from jax.experimental import pallas as pl
from jax.experimental.pallas import tpu as pltpu
from jax.sharding import Mesh, PartitionSpec as P

SPAN = 16
EXTENT = 18
WEIGHT = float(SPAN) ** -1.5
PAIRS = 336
POINTS = 336
GROUP = ("y", "x", "low", "core")
PLANE = ("y", "x", "core")
LINE = ("high", "low")
LINE_SIZE = 32
WINDOW_FLOPS = 1000000000
PLANE_SIZE = 32


def iota(shape, dim):
    return lax.broadcasted_iota(jnp.int32, shape, dim)


def split(value):
    high = value.astype(jnp.bfloat16)
    low = (value - high.astype(jnp.float32)).astype(jnp.bfloat16)
    return high, low


def dot3(left, right, dims):
    (lh, ll), (rh, rl) = left, right

    def one(a, b):
        return lax.dot_general(a, b, (dims, ((), ())), preferred_element_type=jnp.float32)

    return one(lh, rh) + (one(lh, rl) + one(ll, rh))


def exact(left, right, dims=((1,), (0,))):
    return lax.dot_general(
        left, right, (dims, ((), ())),
        precision=lax.Precision.HIGHEST, preferred_element_type=jnp.float32,
    )


def point_index(shape, dim):
    row = iota(shape, dim)
    own = row < 256
    plane = row < 288
    far = row >= 312
    x_side = jnp.where(row < 272, 0, EXTENT - 1)
    x = jnp.where(own, (row >> 4) + 1, jnp.where(plane, x_side, row - jnp.where(far, 312, 288)))
    y = jnp.where(own | plane, (row & 15) + 1, jnp.where(far, EXTENT - 1, 0))
    return x, y


def pair_index(shape, dim):
    pair = iota(shape, dim)
    first = (pair * 3641) >> 16
    return first, pair - EXTENT * first


def message_kernel(
    even_ref, labels_hbm, residual_hbm, out_ref, inner_ref, outer_ref, labels_ref, residual_ref, sems
):
    copies = [pltpu.make_async_copy(residual_hbm.at[v], residual_ref.at[v], sems.at[v]) for v in range(2)]
    copies.append(pltpu.make_async_copy(labels_hbm, labels_ref, sems.at[2]))
    for copy in copies:
        copy.start()
    copies[2].wait()
    lane = iota((1, 128), 1)
    message = jnp.zeros((1, 128), jnp.float32)
    for slot in range(16):
        j, k = divmod(slot, 8)
        label = labels_ref[0, j : j + 1, k : k + 1].astype(jnp.float32)
        message = jnp.where(lane == slot + 32, label, message)
    even = even_ref[0] != 0
    for v in range(2):
        copies[v].wait()
        sums = jnp.concatenate(
            [
                jnp.sum(
                    jnp.sum(residual_ref[v, :, j * SPAN : (j + 1) * SPAN, :], axis=0),
                    axis=0,
                    keepdims=True,
                )
                for j in range(2)
            ],
            axis=0,
        )
        wide = iota((2, 128), 1) >> 4
        for k in range(8):
            total = jnp.sum(jnp.where(wide == k, sums, 0.0), axis=1, keepdims=True)
            for j in range(2):
                slot = v * 16 + j * 8 + k
                message = jnp.where(lane == slot, total[j : j + 1] * WEIGHT, message)
        rows = slice(v * SPAN, (v + 1) * SPAN)
        out_ref[rows, 0, 128:256] = residual_ref[v, :, 2 * SPAN - 1, :]
        out_ref[rows, 0, 256:384] = residual_ref[v, :, 0, :]
        first, last = residual_ref[v, 0], residual_ref[v, SPAN - 1]
        inner_ref[v, 0] = jnp.where(even, last, first)
        outer_ref[v, 0] = jnp.where(even, first, last)
    out_ref[:, 0, 0:128] = jnp.broadcast_to(message, (LINE_SIZE, 128))


def send_messages(even, labels, residual):
    vectors, _, span_y, span_z = residual.shape
    side = jax.ShapeDtypeStruct((vectors, 1, span_y, span_z), jnp.float32)
    return pl.pallas_call(
        message_kernel,
        out_shape=[jax.ShapeDtypeStruct((LINE_SIZE, 1, 384), jnp.float32), side, side],
        in_specs=[pl.BlockSpec(memory_space=pltpu.SMEM)] + [pl.BlockSpec(memory_space=pl.ANY)] * 2,
        out_specs=[pl.BlockSpec(memory_space=pltpu.VMEM)] * 3,
        scratch_shapes=[
            pltpu.VMEM(labels.shape, jnp.int32),
            pltpu.VMEM(residual.shape, jnp.float32),
            pltpu.SemaphoreType.DMA((3,)),
        ],
    )(even, labels, residual)


def scatter_kernel(spots_ref, parts_ref, out_ref):
    slots = jnp.transpose(parts_ref[:, 0, 0:128])
    slots = jnp.concatenate([slots, jnp.zeros((128, 96), jnp.float32)], axis=1)
    quarter = iota((4, 128), 1) >> 5

    def along_lanes(begin):
        total = slots[begin : begin + 4]
        for q in range(1, 4):
            part = pltpu.roll(slots[begin + 4 * q : begin + 4 * q + 4], 32 * q, 1)
            total = jnp.where(quarter == q, part, total)
        return total

    first, second, label = (along_lanes(begin) for begin in (0, 16, 32))
    label = label.astype(jnp.int32)
    row = iota((SPAN, 128), 0)
    block = (row & 7) + (spots_ref[0] >> 3) * 8
    column = iota((128, 128), 0)
    total = jnp.zeros((SPAN, 128), jnp.float32)
    for g in range(4):
        here = (label[g : g + 1] >> 7) == block
        values = jnp.where(row < 8, first[g : g + 1], second[g : g + 1])
        values = jnp.where(here, values, 0.0)
        places = jnp.where((label[g : g + 1] & 127) == column, 1.0, 0.0)
        total = total + exact(values, places, ((1,), (1,)))
    out_ref[...] = jnp.broadcast_to(total[None], out_ref.shape)


def terms_kernel(spots_ref, parts_ref, line_ref, x_low_ref, x_high_ref, matrix_ref, out_ref):
    rhs = jnp.sum(parts_ref[...], axis=0)
    lane = iota((SPAN, 128), 1) - iota((SPAN, 128), 0)
    place = (spots_ref[0] & 3) * 32
    message = jnp.zeros((1, 128), jnp.float32)
    for v in range(2):
        total = jnp.zeros((SPAN, 128), jnp.float32)
        for block in range(8):
            row = v * 8 + block
            total = total + matrix_ref[:, block * 128 : (block + 1) * 128] * rhs[row : row + 1]
        column = jnp.sum(total, axis=1, keepdims=True)
        here = lane == place + SPAN * v
        message = message + jnp.sum(jnp.where(here, column, 0.0), axis=0, keepdims=True)
    out_ref[:, 0, 0:128] = jnp.broadcast_to(message, (LINE_SIZE, 128))
    out_ref[0:8, 0, 128:256] = line_ref[24:32, 0, 128:256]
    out_ref[8:32, 0, 128:256] = line_ref[0:24, 0, 128:256]
    out_ref[0:24, 0, 256:384] = line_ref[8:32, 0, 256:384]
    out_ref[24:32, 0, 256:384] = line_ref[0:8, 0, 256:384]
    out_ref[:, 0, 384:896] = jnp.zeros((LINE_SIZE, 512), jnp.float32)
    for spot, edge in ((1, 0), (2, 2 * SPAN - 1)):
        corners = [
            side_ref[v, 0, edge : edge + 1, :] for v in range(2) for side_ref in (x_low_ref, x_high_ref)
        ]
        out_ref[spots_ref[spot], :, 384:896] = jnp.concatenate(corners, axis=1)


def prepare_kernel(
    residual_ref, x_low_ref, x_high_ref, horiz_ref, high_ref, low_ref, hat_ref, box_ref
):
    x_of, y_of = point_index((POINTS, EXTENT), 0)
    mode = iota((POINTS, EXTENT), 1)
    pair_a, pair_b = pair_index((EXTENT, PAIRS), 1)
    table = iota((EXTENT, PAIRS), 0)
    pick_a = jnp.where(pair_a == table, 1.0, 0.0)
    pick_b = jnp.where((pair_b == table) & (pair_a < EXTENT), 1.0, 0.0)
    rows_x = exact(jnp.where(x_of == mode, 1.0, 0.0), exact(horiz_ref[0], pick_a))
    rows_y = exact(jnp.where(y_of == mode, 1.0, 0.0), exact(horiz_ref[1], pick_b))
    high, low = split(rows_x * rows_y)
    high_ref[...] = high
    low_ref[...] = low
    for v in range(2):
        for j in range(2):
            lanes = slice(128 * (2 * v + j), 128 * (2 * v + j + 1))
            ys = slice(j * SPAN, (j + 1) * SPAN)
            box_ref[0:256, lanes] = residual_ref[v, :, ys, :].reshape(256, 128)
            box_ref[256:272, lanes] = x_low_ref[v, 0, ys, :]
            box_ref[272:288, lanes] = x_high_ref[v, 0, ys, :]
    hat_ref[...] = dot3((high[:288], low[:288]), split(box_ref[...]), ((0,), (0,)))


def finish_kernel(
    spots_ref, residual_ref, x_low_ref, x_high_ref, line_parts_ref, high_ref, low_ref, hat_ref,
    horiz_values_ref, upward_ref, upward_values_ref,
    out_ref, box_ref, line_ref, line_values_ref,
):
    line_ref[...] = jnp.zeros_like(line_ref)
    for k in range(8):
        begin = 16 * k - 1
        skip = 1 if k == 0 else 0
        stop = 17 if k == 7 else 18
        line_ref[begin + skip : begin + stop, 18 * k : 18 * k + 18] = upward_ref[k, skip:stop, :]
        line_values_ref[0:1, 18 * k : 18 * k + 18] = upward_values_ref[k : k + 1, :]
    line = line_ref[...]
    z = iota((128, 144), 0)
    layer, _ = pair_index((128, 144), 1)
    line_own = split(jnp.where((z >> 4) == layer, line, 0.0))
    line = split(line)

    pair_first, pair_second = pair_index((PAIRS, EXTENT), 0)
    table = iota((PAIRS, EXTENT), 1)
    values = jnp.sum(
        jnp.where(pair_first == table, horiz_values_ref[0:1, :], 0.0)
        + jnp.where(pair_second == table, horiz_values_ref[1:2, :], 0.0),
        axis=1,
        keepdims=True,
    )
    inverse = 1.0 / (values + line_values_ref[...])

    for v in range(2):
        rows = slice(SPAN * v, SPAN * v + SPAN)
        for j in range(2):
            lanes = slice(128 * (2 * v + j), 128 * (2 * v + j + 1))
            for begin, edge, spot in ((0, 15, 1), (24, 16, 2)):
                box_ref[begin + 16 : begin + 24, lanes] = jnp.zeros((8, 128), jnp.float32)
                if (edge == 15) == (j == 0):
                    corner = line_parts_ref[spots_ref[spot]]
                    first = 128 * (3 + 2 * v)
                    side = slice(128 * spot, 128 * (spot + 1))
                    box_ref[begin : begin + 1, lanes] = corner[:, first : first + 128]
                    box_ref[begin + 1 : begin + 17, lanes] = line_parts_ref[rows, 0, side]
                    box_ref[begin + 17 : begin + 18, lanes] = corner[:, first + 128 : first + 256]
                else:
                    box_ref[begin : begin + 1, lanes] = x_low_ref[v, 0, edge : edge + 1, :]
                    box_ref[begin + 1 : begin + 17, lanes] = residual_ref[v, :, edge, :]
                    box_ref[begin + 17 : begin + 18, lanes] = x_high_ref[v, 0, edge : edge + 1, :]
    sides = (high_ref[288:336, :], low_ref[288:336, :])
    own = (high_ref[0:256, :], low_ref[0:256, :])
    all_hat = hat_ref[...] + dot3(sides, split(box_ref[...]), ((0,), (0,)))

    for part in range(4):
        hat = dot3(split(all_hat[:, 128 * part : 128 * (part + 1)]), line, ((1,), (0,)))
        back = dot3(split(hat * inverse), line_own, ((1,), (1,)))
        solved = dot3(own, split(back), ((1,), (0,)))
        v, j = divmod(part, 2)
        out_ref[v, :, j * SPAN : (j + 1) * SPAN, :] = solved.reshape(SPAN, SPAN, 128)


def rows_kernel(parts_ref, out_ref):
    rows = jnp.sum(parts_ref[:, 0, 0:128].reshape(4, 2, 4, 128), axis=(0, 2))
    out_ref[...] = jnp.broadcast_to(rows[None], out_ref.shape)


def merge_kernel(labels_ref, local_ref, coarse_ref, out_ref):
    lane = iota((1, 128), 1)
    for j in range(2):
        updates = [jnp.zeros((1, 128), jnp.float32)] * 2
        for k in range(8):
            label = labels_ref[0, j, k]
            block = ((label >> 8) << 1) | ((label >> 4) & 1)
            place = (((label >> 5) & 3) << 5) | (label & 15)
            row = coarse_ref[block, pl.ds((label >> 7) & 1, 1), :]
            for v in range(2):
                here = lane == place + SPAN * v
                value = jnp.sum(jnp.where(here, row, 0.0), axis=1, keepdims=True)
                updates[v] = jnp.where((lane >> 4) == k, value * WEIGHT, updates[v])
        ys = slice(j * SPAN, (j + 1) * SPAN)
        for v in range(2):
            out_ref[v, :, ys, :] = local_ref[v, :, ys, :] + updates[v][None]


def call(kernel, out_shape, scalars, arrays, scratch=(), cost=None):
    if not isinstance(out_shape, list):
        out_shape = jax.ShapeDtypeStruct(out_shape, jnp.float32)
    return pl.pallas_call(
        kernel,
        out_shape=out_shape,
        in_specs=[pl.BlockSpec(memory_space=pltpu.SMEM)] * len(scalars)
        + [pl.BlockSpec(memory_space=pltpu.VMEM)] * len(arrays),
        out_specs=jax.tree.map(lambda _: pl.BlockSpec(memory_space=pltpu.VMEM), out_shape),
        scratch_shapes=list(scratch),
        compiler_params=pltpu.CompilerParams(vmem_limit_bytes=40 << 20),
        cost_estimate=cost,
    )(*scalars, *arrays)


def on_device(
    residual, horiz_vectors, horiz_values, upward_eigen_tables, upward_eigen_values,
    aggregate_map, coarse_inverse,
):
    labels = aggregate_map
    even = lax.axis_index("core") == 0
    spot = lax.axis_index("high") * 8 + lax.axis_index("low")
    spots = (spot + jnp.array([0, 24, 8], jnp.int32)) % LINE_SIZE
    barrier = lax.optimization_barrier

    parts, inner, outer = send_messages(even.astype(jnp.int32).reshape(1), labels, residual)
    parts, inner, outer = barrier((parts, inner, outer))
    line_parts = lax.all_to_all(parts, LINE, 0, 0)
    inner = lax.ppermute(inner, GROUP, [(i, i ^ 1) for i in range(256)])
    outer = lax.ppermute(outer, GROUP, [(i, (i + i % 2 * 2 - 1) % 256) for i in range(256)])
    x_low, x_high = jnp.where(even, outer, inner), jnp.where(even, inner, outer)

    dense = call(scatter_kernel, (PLANE_SIZE, 16, 128), [spots], [line_parts])
    plane_parts = lax.all_to_all(dense, PLANE, 0, 0)
    table = jax.ShapeDtypeStruct((POINTS, PAIRS), jnp.bfloat16)
    prepared = call(
        prepare_kernel,
        [table, table, jax.ShapeDtypeStruct((PAIRS, 512), jnp.float32)],
        [], [residual, x_low, x_high, horiz_vectors],
        [pltpu.VMEM((288, 512), jnp.float32)],
        pl.CostEstimate(flops=WINDOW_FLOPS, transcendentals=0, bytes_accessed=1 << 20),
    )
    plane_parts, prepared, x_low, x_high = barrier((plane_parts, prepared, x_low, x_high))
    terms = call(
        terms_kernel, (LINE_SIZE, 1, 896), [spots],
        [plane_parts, line_parts, x_low, x_high, coarse_inverse],
    )
    row_parts = lax.all_to_all(terms, LINE, 0, 0)
    coarse = lax.all_to_all(call(rows_kernel, (PLANE_SIZE, 2, 128), [], [row_parts]), PLANE, 0, 0)
    local = call(
        finish_kernel, residual.shape, [spots],
        [residual, x_low, x_high, row_parts, *prepared, horiz_values,
         upward_eigen_tables, upward_eigen_values],
        [pltpu.VMEM((48, 512), jnp.float32), pltpu.VMEM((128, 144), jnp.float32),
         pltpu.VMEM((1, 144), jnp.float32)],
    )
    return call(merge_kernel, residual.shape, [labels], [local, coarse])


def solution(mesh):
    fine = Mesh(mesh.devices.reshape(4, 4, 8, 2, 4), ("y", "x", "low", "core", "high"))
    in_specs = (
        P(None, GROUP, "high", None),
        P(), P(), P(), P(),
        P(GROUP, "high", None),
        P(GROUP, "high"),
    )
    return jax.shard_map(
        on_device, mesh=fine, in_specs=in_specs, out_specs=in_specs[0], check_vma=False
    )
```
